512 devices in a mesh: date: 32 (over x, z), col: 16 (over y, core).
Axes of the slice: x: 4, y: 8, z: 8, core: 2. Of those that a mesh axis runs over, the one named last changes fastest.
Arguments:
- slc: float32 [2, 32, 128, 8192], P(None, 'date', None, 'col'), may hold values from -80 to 80
- offsets: int32 [32, 4], replicated, may hold values from 0 to 6, as said below
Outputs:
- interferogram: float32 [2, 32, 4, 32, 512], P(None, 'date', None, None, 'col')
- coherence: float32 [32, 4, 32, 512], P('date', None, None, 'col')
The draws below stay inside these ranges and needn't reach their ends.
Inputs may be any that keep to these rules, and one draw needn't show every extreme that they name: Row d lists the offsets of the pairs whose reference date is d; 0 marks an empty slot, the nonzero entries of a row are distinct, and d plus each offset is at most 31. Date 0 has 4 pairs, one of offset 6.
All inputs are finite; a program needn't handle non-finite values.
Results may differ from the reference program's by a relative error of at most 0.0003.
Values sent between devices are 32-bit elements; how exact they have to be, the bound alone decides.
No kernel may reach another device: no remote copies, remote signals or barrier semaphores. Data moves between devices by JAX's collectives and lax.ppermute only.
A program may use at most 64 MiB of HBM per device.

```python
import math
import jax
import jax.numpy as jnp
from jax import lax

SLOTS = 4
MAX_OFFSET = 6
DATES = 32
ROWS = 128
COLS = 8192


def draw_slc(key, part):
    subkeys = jax.random.split(key, 4)
    full_shape = (2, DATES, ROWS, COLS)
    common = jnp.clip(jax.random.normal(subkeys[0], (2, 1, ROWS, COLS), jnp.float32), -6.0, 6.0)
    noise = jnp.clip(jax.random.normal(subkeys[1], full_shape, jnp.float32), -6.0, 6.0)
    mixing = jnp.exp(jax.random.uniform(subkeys[2], (1, DATES, ROWS, COLS), jnp.float32, math.log(0.3), math.log(3.0)))
    amplitude = jnp.exp(jax.random.uniform(subkeys[3], (1, 1, ROWS, COLS), jnp.float32, math.log(0.3), math.log(3.0)))
    return (amplitude * (common + mixing * noise)).astype(jnp.float32)


def draw_offsets(key, part):
    subkeys = jax.random.split(key, 2)
    scores = jax.random.randint(subkeys[0], (DATES, MAX_OFFSET), 0, 1 << 20)
    scores = scores * MAX_OFFSET + jnp.arange(MAX_OFFSET, dtype=jnp.int32)[None, :]
    ranked = jnp.argsort(scores, axis=1)[:, :SLOTS]
    chosen = (ranked + 1).astype(jnp.int32)
    kept = jax.random.randint(subkeys[1], (DATES, SLOTS), 0, 4) > 0
    first_row = (MAX_OFFSET - jnp.arange(SLOTS, dtype=jnp.int32)).astype(jnp.int32)
    date_rows = jnp.arange(DATES, dtype=jnp.int32)[:, None]
    chosen = jnp.where(date_rows == 0, first_row[None, :], chosen)
    kept = kept | (date_rows == 0)
    kept = kept & (date_rows + chosen <= DATES - 1)
    return jnp.where(kept, chosen, 0).astype(jnp.int32)


def setup_inputs(seed: int = 0) -> dict:
    streams_of = jax.random.split(jax.random.key(seed), 3)
    slc = draw_slc(jax.random.fold_in(streams_of[2], 71), 0)
    offsets = draw_offsets(jax.random.fold_in(streams_of[2], 71), 0)
    return dict(slc=slc, offsets=offsets)


epsilon = 1e-06

def look_sums(master_real, master_imag, partner_real, partner_imag, live_mask):
    prod_real = master_real * partner_real + master_imag * partner_imag
    prod_imag = master_imag * partner_real - master_real * partner_imag
    power_master = master_real * master_real + master_imag * master_imag
    power_partner = partner_real * partner_real + partner_imag * partner_imag
    power_master = jnp.broadcast_to(power_master, prod_real.shape)
    stacked = jnp.stack([prod_real, prod_imag, power_master, power_partner])
    full_shape = stacked.shape
    blocks = stacked.reshape(full_shape[:-2] + (full_shape[-2] // 4, 4, full_shape[-1] // 16, 16))
    looked = lax.optimization_barrier(jnp.sum(blocks, axis=(-3, -1))) / 64.0
    return looked * live_mask

def coherence_of(padded):
    row_count = padded.shape[-2] - 2
    col_count = padded.shape[-1] - 2
    window_sum = padded[..., 0:row_count, 0:col_count]
    for down_step in range(3):
        for side_step in range(3):
            if down_step or side_step:
                window_sum = window_sum + padded[..., down_step:down_step + row_count, side_step:side_step + col_count]
    magnitude = jnp.sqrt(window_sum[0] * window_sum[0] + window_sum[1] * window_sum[1])
    return magnitude / (jnp.sqrt(window_sum[2] * window_sum[3]) + epsilon)

def reference(slc, offsets):
    date_count = slc.shape[1]

    def one_date(reference_date):
        date_offsets = offsets[reference_date]
        live_mask = (date_offsets > 0).astype(jnp.float32)
        partner_index = jnp.clip(reference_date + date_offsets, 0, date_count - 1).astype(jnp.int32)
        master = slc[:, reference_date]
        partner = jnp.take(slc, partner_index, axis=1)
        return look_sums(master[0], master[1], partner[0], partner[1], live_mask[:, None, None])
    looked = lax.map(one_date, jnp.arange(date_count, dtype=jnp.int32))
    looked = jnp.moveaxis(looked, 0, 1)
    padded = jnp.pad(looked, ((0, 0), (0, 0), (0, 0), (1, 1), (1, 1)))
    return (looked[0:2], coherence_of(padded))
```

```python
import functools

import jax
import jax.numpy as jnp
from jax import lax
from jax.experimental import pallas as pl
from jax.experimental.pallas import tpu as pltpu
from jax.sharding import PartitionSpec as P

SLOTS = 4
DATES = 32
MAPS = 3 * SLOTS + 1
GROUPS = 2 * MAPS
HALO_LANE = 32

epsilon = 1e-06


def three_parts(value):
    high = value.astype(jnp.bfloat16)
    rest = value - high.astype(jnp.float32)
    middle = rest.astype(jnp.bfloat16)
    low = (rest - middle.astype(jnp.float32)).astype(jnp.bfloat16)
    return high, middle, low


def looks_kernel(offs_smem, offs_ref, tiles_ref, looks_ref, edge_ref, prod, power, stack):
    half = lax.rem(lax.axis_index("date"), 2)

    def powers(d, carry):
        for t in range(2):
            real = tiles_ref[d, 0, t]
            imag = tiles_ref[d, 1, t]
            value = real * real + imag * imag
            power[t, d] = value
            prod[t, MAPS - 1, pl.ds(pl.multiple_of(d * 8, 8), 8), :] = value
        return carry

    lax.fori_loop(0, DATES, powers, 0, unroll=4)

    def pairs(d, carry):
        rows = pl.ds(pl.multiple_of(d * 8, 8), 8)
        for t in range(2):
            master_real = tiles_ref[d, 0, t]
            master_imag = tiles_ref[d, 1, t]
            for j in range(SLOTS):
                p = jnp.minimum(d + offs_smem[d * SLOTS + j], DATES - 1)
                partner_real = tiles_ref[p, 0, t]
                partner_imag = tiles_ref[p, 1, t]
                prod[t, j, rows, :] = master_real * partner_real + master_imag * partner_imag
                prod[t, SLOTS + j, rows, :] = master_imag * partner_real - master_real * partner_imag
                prod[t, 2 * SLOTS + j, rows, :] = power[t, p]
        return carry

    lax.fori_loop(0, DATES, pairs, 0, unroll=2)

    live = (offs_ref[...] > 0).astype(jnp.float32) / 64.0
    lives = [jnp.broadcast_to(live[:, j : j + 1], (DATES, 128)) for j in range(SLOTS)]
    for m in range(MAPS):
        scale = lives[m % SLOTS] if m < MAPS - 1 else 1.0 / 64.0
        for r in range(2):
            g = 2 * m + r
            for t in range(2):
                total = prod[t, m, pl.ds(4 * r, DATES, stride=8), :]
                for i in range(1, 4):
                    total = total + prod[t, m, pl.ds(4 * r + i, DATES, stride=8), :]
                for q, part in enumerate(three_parts(total * scale)):
                    lanes = 128 * (3 * t + q)
                    stack[pl.ds(DATES * g, DATES), lanes : lanes + 128] = part

    lane = lax.broadcasted_iota(jnp.int32, (768, 256), 0)
    place = lax.broadcasted_iota(jnp.int32, (768, 256), 1)
    look = (lane // 384) * 8 + (lane % 128) // 16
    want = jnp.where(place < 128, place % 16, half * 15)
    sums = (look == want).astype(jnp.bfloat16)
    out = jnp.dot(stack[...], sums, preferred_element_type=jnp.float32)
    lanes = lax.broadcasted_iota(jnp.int32, (DATES, 128), 1)
    edge = jnp.zeros((DATES, 128), jnp.float32)
    for k in range(4):
        block = jnp.zeros((DATES, 128), jnp.float32)
        for g in range(8 * k, min(8 * k + 8, GROUPS)):
            rows = slice(DATES * g, DATES * g + DATES)
            block = jnp.where(lanes // 16 == g - 8 * k, out[rows, :128], block)
            edge = jnp.where(lanes == HALO_LANE + g, out[rows, 128:], edge)
        looks_ref[pl.ds(k, DATES, stride=4), :] = block
    edge_ref[...] = edge


def local_looks(offsets, tiles):
    vmem = pl.BlockSpec(memory_space=pltpu.VMEM)
    return pl.pallas_call(
        looks_kernel,
        out_shape=(
            jax.ShapeDtypeStruct((4 * DATES, 128), jnp.float32),
            jax.ShapeDtypeStruct((DATES, 128), jnp.float32),
        ),
        in_specs=[pl.BlockSpec(memory_space=pltpu.SMEM), vmem, vmem],
        out_specs=(vmem, vmem),
        scratch_shapes=[
            pltpu.VMEM((2, MAPS, 8 * DATES, 128), jnp.float32),
            pltpu.VMEM((2, DATES, 8, 128), jnp.float32),
            pltpu.VMEM((GROUPS * DATES, 768), jnp.bfloat16),
        ],
        name="looks",
    )(offsets.reshape(-1), offsets, tiles)


def with_edge_kernel(looks_ref, edge_ref, out_ref):
    rows = pl.ds(3, DATES, stride=4)
    out_ref[...] = looks_ref[...]
    out_ref[rows, :] = looks_ref[rows, :] + edge_ref[...]


def with_edge(looks, edge):
    vmem = pl.BlockSpec(memory_space=pltpu.VMEM)
    return pl.pallas_call(
        with_edge_kernel,
        out_shape=jax.ShapeDtypeStruct((4 * DATES, 128), jnp.float32),
        in_specs=[vmem, vmem],
        out_specs=vmem,
        name="with_edge",
    )(looks, edge)


def finish_kernel(offs_smem, looks_ref, inter_ref, coh_ref):
    date = lax.axis_index("date")
    lanes = lax.broadcasted_iota(jnp.int32, (16, 128), 1)
    blocks = [[looks_ref[pl.ds(4 * half + k, 16, stride=8), :] for k in range(4)] for half in range(2)]

    def cells(m, r):
        g = 2 * m + r
        k, at = g // 8, 16 * (g % 8)
        value = jnp.zeros((16, 128), jnp.float32)
        for half in range(2):
            piece = pltpu.roll(blocks[half][k], (16 * half - at) % 128, 1)
            value = jnp.where(lanes // 16 == half, piece, value)
        left = pltpu.roll(blocks[0][3], (127 - HALO_LANE - g) % 128, 1)
        right = pltpu.roll(blocks[1][3], (32 - HALO_LANE - g) % 128, 1)
        return jnp.where(lanes == 127, left, jnp.where(lanes == 32, right, value))

    row = lax.broadcasted_iota(jnp.int32, (16, 128), 0)

    def window(m):
        across = []
        for r in range(2):
            value = cells(m, r)
            if m < 2 * SLOTS:
                inter_ref[m // SLOTS, 0, m % SLOTS, pl.ds(r, 16, stride=2), :] = value[:, :32]
            across.append(value + pltpu.roll(value, 1, 1) + pltpu.roll(value, 127, 1))
        both = across[0] + across[1]
        above = jnp.where(row == 0, 0.0, pltpu.roll(across[1], 1, 0))
        below = jnp.where(row == 15, 0.0, pltpu.roll(across[0], 15, 0))
        return both + above, both + below

    own = window(MAPS - 1)
    for j in range(SLOTS):
        live = (offs_smem[date * SLOTS + j] > 0).astype(jnp.float32)
        real, imag, partner = window(j), window(SLOTS + j), window(2 * SLOTS + j)
        for r in range(2):
            magnitude = jnp.sqrt(real[r] * real[r] + imag[r] * imag[r])
            value = magnitude / (jnp.sqrt((own[r] * live) * partner[r]) + epsilon)
            coh_ref[0, j, pl.ds(r, 16, stride=2), :] = value[:, :32]


def finish(offsets, looks):
    vmem = pl.BlockSpec(memory_space=pltpu.VMEM)
    return pl.pallas_call(
        finish_kernel,
        out_shape=(
            jax.ShapeDtypeStruct((2, 1, SLOTS, 32, 32), jnp.float32),
            jax.ShapeDtypeStruct((1, SLOTS, 32, 32), jnp.float32),
        ),
        in_specs=[pl.BlockSpec(memory_space=pltpu.SMEM), vmem],
        out_specs=(vmem, vmem),
        name="finish",
    )(offsets.reshape(-1), looks)


def edge_pairs(dates, cols):
    pairs = []
    for block in range(dates // 2):
        for c in range(1, cols):
            here, there = 2 * block * cols + c, (2 * block + 1) * cols + c - 1
            pairs += [(here, there), (there, here)]
    return pairs


def shards(slc, offsets):
    tiles = slc.reshape(2, 16, 8, 2, 2, 128).transpose(1, 3, 0, 4, 2, 5).reshape(DATES, 2, 2, 8, 128)
    tiles = lax.all_to_all(tiles, "date", 0, 0, tiled=True)
    looks, edge = local_looks(offsets, tiles)
    edge = lax.ppermute(edge, ("date", "col"), edge_pairs(DATES, lax.axis_size("col")))
    looks = with_edge(looks, edge)
    looks = lax.all_to_all(looks.reshape(DATES, 4, 128), "date", 0, 0, tiled=True)
    return finish(offsets, looks.reshape(4 * DATES, 128))


def solution(mesh):
    placed = (P(None, "date", None, "col"), P())
    return jax.shard_map(
        shards,
        mesh=mesh,
        in_specs=placed,
        out_specs=(P(None, "date", None, None, "col"), P("date", None, None, "col")),
        check_vma=False,
    )
```

```python
import jax
import jax.numpy as jnp
from jax import lax
from jax.experimental import pallas as pl
from jax.experimental.pallas import tpu as pltpu
from jax.sharding import PartitionSpec as P

SLOTS = 4
DATES = 32
MAX_OFFSET = 6
MAPS = 3 * SLOTS + 1
GROUPS = 2 * MAPS
HALO_LANE = 32
STAGES = 4

epsilon = 1e-06

VMEM = pl.BlockSpec(memory_space=pltpu.VMEM)
ANY = pl.BlockSpec(memory_space=pl.ANY)


def in_vmem(value):
    return pltpu.with_memory_space_constraint(value, pltpu.VMEM)


def odd_col():
    return lax.rem(lax.axis_index("col"), 2)


def own_half():
    return lax.rem(lax.axis_index("date") + lax.axis_index("col"), 2)


def two_parts(value):
    high = value.astype(jnp.bfloat16)
    return high, (value - high.astype(jnp.float32)).astype(jnp.bfloat16)


def pieces_kernel(slc_ref, out_ref, sems):
    odd = odd_col()
    copies = [
        pltpu.make_async_copy(
            slc_ref.at[p, :, half],
            out_ref.at[:, jnp.bitwise_xor(odd, half), p],
            sems.at[p, half],
        )
        for p in range(2)
        for half in range(2)
    ]
    for copy in copies:
        copy.start()
    for copy in copies:
        copy.wait()


def pieces(slc):
    tiles = slc.reshape(2, 16, 8, 2, 2, 128).transpose(0, 1, 3, 4, 2, 5)
    return pl.pallas_call(
        pieces_kernel,
        out_shape=pltpu.VMEM((16, 2, 2, 2, 8, 128), jnp.float32),
        in_specs=[ANY],
        out_specs=VMEM,
        scratch_shapes=[pltpu.SemaphoreType.DMA((2, 2))],
        name="pieces",
    )(tiles)


def edge_kernel(offs_ref, tiles_ref, edge_ref, shifted, stack):
    half = own_half()
    lanes = lax.broadcasted_iota(jnp.int32, (DATES, 128), 1)
    packed = []
    for p in range(2):
        value = jnp.zeros((DATES, 128), jnp.float32)
        for i in range(8):
            row = tiles_ref[pl.ds(16 * p + 8 * half + i, DATES, stride=32), :]
            value = jnp.where(lanes // 16 == i, pltpu.roll(row, 16 * (half + i), 1), value)
        packed.append(value)
    packed.append(packed[0] * packed[0] + packed[1] * packed[1])
    for q in range(3):
        shifted[q, 0:DATES, :] = packed[q]
        shifted[q, DATES : DATES + 8, :] = jnp.zeros((8, 128), jnp.float32)
    offs = offs_ref[...]
    looks = [None] * (MAPS - 1) + [packed[2]]
    for j in range(SLOTS):
        offset = jnp.broadcast_to(offs[:, j : j + 1], (DATES, 128))
        partner = [jnp.zeros((DATES, 128), jnp.float32)] * 3
        for step in range(1, MAX_OFFSET + 1):
            partner = [jnp.where(offset == step, shifted[q, step : step + DATES, :], partner[q]) for q in range(3)]
        looks[j] = packed[0] * partner[0] + packed[1] * partner[1]
        looks[SLOTS + j] = packed[1] * partner[0] - packed[0] * partner[1]
        looks[2 * SLOTS + j] = partner[2]
    for m in range(MAPS):
        for q, part in enumerate(two_parts(looks[m] / 64.0)):
            stack[DATES * m : DATES * m + DATES, 128 * q : 128 * q + 128] = part
    lane = lax.broadcasted_iota(jnp.int32, (256, 128), 0)
    place = lax.broadcasted_iota(jnp.int32, (256, 128), 1)
    sums = ((lane % 128) // 64 == place % 2).astype(jnp.bfloat16)
    out = jnp.dot(stack[...], sums, preferred_element_type=jnp.float32)
    edge = jnp.zeros((DATES, 128), jnp.float32)
    for m in range(MAPS):
        edge = jnp.where((lanes - HALO_LANE) // 2 == m, out[DATES * m : DATES * m + DATES, :], edge)
    edge_ref[...] = jnp.where(lanes >= HALO_LANE, edge, 0.0)


def edge_looks(offsets, tiles):
    return pl.pallas_call(
        edge_kernel,
        out_shape=pltpu.VMEM((DATES, 128), jnp.float32),
        in_specs=[VMEM, VMEM],
        out_specs=VMEM,
        scratch_shapes=[
            pltpu.VMEM((3, DATES + 8, 128), jnp.float32),
            pltpu.VMEM((MAPS * DATES, 256), jnp.bfloat16),
        ],
        name="edge_looks",
    )(in_vmem(offsets), in_vmem(tiles))


def looks_kernel(offs_smem, offs_ref, tiles_ref, looks_ref, prod, power, stack):
    def tile(d, p, t):
        return tiles_ref[pl.ds(pl.multiple_of(d * 32 + 16 * p + 8 * t, 8), 8), :]

    def powers(d, carry):
        for t in range(2):
            real, imag = tile(d, 0, t), tile(d, 1, t)
            value = real * real + imag * imag
            power[t, d] = value
            prod[t, MAPS - 1, pl.ds(pl.multiple_of(d * 8, 8), 8), :] = value
        return carry

    lax.fori_loop(0, DATES, powers, 0, unroll=4)

    def pairs(d, carry):
        rows = pl.ds(pl.multiple_of(d * 8, 8), 8)
        for t in range(2):
            master_real, master_imag = tile(d, 0, t), tile(d, 1, t)
            for j in range(SLOTS):
                p = jnp.minimum(d + offs_smem[d, j], DATES - 1)
                partner_real, partner_imag = tile(p, 0, t), tile(p, 1, t)
                prod[t, j, rows, :] = master_real * partner_real + master_imag * partner_imag
                prod[t, SLOTS + j, rows, :] = master_imag * partner_real - master_real * partner_imag
                prod[t, 2 * SLOTS + j, rows, :] = power[t, p]
        return carry

    lax.fori_loop(0, DATES, pairs, 0, unroll=2)

    live = (offs_ref[...] > 0).astype(jnp.float32) / 64.0
    lives = [jnp.broadcast_to(live[:, j : j + 1], (DATES, 128)) for j in range(SLOTS)]
    for m in range(MAPS):
        scale = lives[m % SLOTS] if m < MAPS - 1 else 1.0 / 64.0
        for r in range(2):
            g = 2 * m + r
            for t in range(2):
                total = prod[t, m, pl.ds(4 * r, DATES, stride=8), :]
                for i in range(1, 4):
                    total = total + prod[t, m, pl.ds(4 * r + i, DATES, stride=8), :]
                for q, part in enumerate(two_parts(total * scale)):
                    lanes = 128 * (2 * t + q)
                    stack[pl.ds(DATES * g, DATES), lanes : lanes + 128] = part

    lane = lax.broadcasted_iota(jnp.int32, (512, 128), 0)
    place = lax.broadcasted_iota(jnp.int32, (512, 128), 1)
    sums = ((lane // 256) * 8 + (lane % 128) // 16 == place % 16).astype(jnp.bfloat16)
    out = jnp.dot(stack[...], sums, preferred_element_type=jnp.float32)
    lanes = lax.broadcasted_iota(jnp.int32, (DATES, 128), 1)
    for k in range(4):
        block = jnp.zeros((DATES, 128), jnp.float32)
        for g in range(8 * k, min(8 * k + 8, GROUPS)):
            block = jnp.where(lanes // 16 == g - 8 * k, out[DATES * g : DATES * g + DATES, :], block)
        looks_ref[pl.ds(k, DATES, stride=4), :] = block


def local_looks(offsets, tiles):
    return pl.pallas_call(
        looks_kernel,
        out_shape=pltpu.VMEM((4 * DATES, 128), jnp.float32),
        in_specs=[pl.BlockSpec(memory_space=pltpu.SMEM), VMEM, VMEM],
        out_specs=VMEM,
        scratch_shapes=[
            pltpu.VMEM((2, MAPS, 8 * DATES, 128), jnp.float32),
            pltpu.VMEM((2, DATES, 8, 128), jnp.float32),
            pltpu.VMEM((GROUPS * DATES, 512), jnp.bfloat16),
        ],
        name="looks",
    )(offsets, in_vmem(offsets), in_vmem(tiles))


def with_edge_kernel(looks_ref, edge_ref, out_ref):
    rows = pl.ds(3, DATES, stride=4)
    out_ref[rows, :] = looks_ref[rows, :] + edge_ref[...]


def with_edge(looks, edge):
    return pl.pallas_call(
        with_edge_kernel,
        out_shape=pltpu.VMEM((4 * DATES, 128), jnp.float32),
        in_specs=[VMEM, VMEM],
        out_specs=VMEM,
        input_output_aliases={0: 0},
        name="with_edge",
    )(in_vmem(looks), in_vmem(edge))


def finish_kernel(offs_ref, looks_ref, inter_ref, coh_ref):
    odd = odd_col()
    lanes = lax.broadcasted_iota(jnp.int32, (16, 128), 1)
    blocks = [
        [looks_ref[pl.ds(4 * jnp.bitwise_xor(odd, half) + k, 16, stride=8), :] for k in range(4)]
        for half in range(2)
    ]

    def cells(m, r):
        g = 2 * m + r
        k, at = g // 8, 16 * (g % 8)
        value = jnp.zeros((16, 128), jnp.float32)
        for half in range(2):
            piece = pltpu.roll(blocks[half][k], (16 * half - at) % 128, 1)
            value = jnp.where(lanes // 16 == half, piece, value)
        left = pltpu.roll(blocks[0][3], (127 - HALO_LANE - g) % 128, 1)
        right = pltpu.roll(blocks[1][3], (32 - HALO_LANE - g) % 128, 1)
        return jnp.where(lanes == 127, left, jnp.where(lanes == 32, right, value))

    row = lax.broadcasted_iota(jnp.int32, (16, 128), 0)

    def window(m):
        across = []
        for r in range(2):
            value = cells(m, r)
            if m < 2 * SLOTS:
                inter_ref[m // SLOTS, 0, m % SLOTS, pl.ds(r, 16, stride=2), :] = value[:, :32]
            across.append(value + pltpu.roll(value, 1, 1) + pltpu.roll(value, 127, 1))
        both = across[0] + across[1]
        above = jnp.where(row == 0, 0.0, pltpu.roll(across[1], 1, 0))
        below = jnp.where(row == 15, 0.0, pltpu.roll(across[0], 15, 0))
        return both + above, both + below

    own = window(MAPS - 1)
    lives = (offs_ref[pl.ds(lax.axis_index("date"), 1), :] > 0).astype(jnp.float32)
    for j in range(SLOTS):
        live = jnp.broadcast_to(lives[:, j : j + 1], (16, 128))
        real, imag, partner = window(j), window(SLOTS + j), window(2 * SLOTS + j)
        for r in range(2):
            magnitude = jnp.sqrt(real[r] * real[r] + imag[r] * imag[r])
            value = magnitude / (jnp.sqrt((own[r] * live) * partner[r]) + epsilon)
            coh_ref[0, j, pl.ds(r, 16, stride=2), :] = value[:, :32]


def finish(offsets, looks):
    return pl.pallas_call(
        finish_kernel,
        out_shape=(
            jax.ShapeDtypeStruct((2, 1, SLOTS, 32, 32), jnp.float32),
            jax.ShapeDtypeStruct((1, SLOTS, 32, 32), jnp.float32),
        ),
        in_specs=[VMEM, VMEM],
        out_specs=(VMEM, VMEM),
        name="finish",
    )(in_vmem(offsets), in_vmem(looks))


def edge_pairs(dates, cols):
    pairs = []
    for c in range(1, cols):
        for d in range(c % 2, dates, 2):
            here, there = d * cols + c, d * cols + c - 1
            pairs += [(here, there), (there, here)]
    return pairs


def shards(slc, offsets):
    tiles, offsets = lax.optimization_barrier((pieces(slc).reshape(DATES, 32, 128), offsets))
    tiles = lax.all_to_all(tiles, "date", 0, 0, tiled=True)
    tiles = tiles.reshape(32 * DATES, 128)
    edge = edge_looks(offsets, tiles)
    edge = lax.ppermute(edge, ("date", "col"), edge_pairs(DATES, lax.axis_size("col")))
    looks = with_edge(local_looks(offsets, tiles), edge)
    looks = lax.all_to_all(looks.reshape(DATES, 4, 128), "date", 0, 0, tiled=True)
    return finish(offsets, looks.reshape(4 * DATES, 128))


def solution(mesh):
    placed = (P(None, "date", None, "col"), P())
    return jax.shard_map(
        shards,
        mesh=mesh,
        in_specs=placed,
        out_specs=(P(None, "date", None, None, "col"), P("date", None, None, "col")),
        check_vma=False,
    )
```

```python
import jax
import jax.numpy as jnp
from jax import lax
from jax.experimental import pallas as pl
from jax.experimental.pallas import tpu as pltpu
from jax.sharding import PartitionSpec as P

SLOTS = 4
DATES = 32
MAX_OFFSET = 6
MAPS = 3 * SLOTS + 1
GROUPS = 2 * MAPS
HALO_LANE = 32

epsilon = 1e-06

VMEM = pl.BlockSpec(memory_space=pltpu.VMEM)
ANY = pl.BlockSpec(memory_space=pl.ANY)


def in_vmem(value):
    return pltpu.with_memory_space_constraint(value, pltpu.VMEM)


def odd_col():
    return lax.rem(lax.axis_index("col"), 2)


def own_half():
    return lax.rem(lax.axis_index("date") + lax.axis_index("col"), 2)


def two_parts(value):
    high = value.astype(jnp.bfloat16)
    return high, (value - high.astype(jnp.float32)).astype(jnp.bfloat16)


def pieces_kernel(slc_ref, slots_ref, out_ref, offs_ref, slots, sems, slots_sem):
    odd = odd_col()
    first = pltpu.make_async_copy(slots_ref, slots, slots_sem)
    first.start()
    copies = [
        pltpu.make_async_copy(
            slc_ref.at[p, :, half],
            out_ref.at[:, jnp.bitwise_xor(odd, half), p],
            sems.at[p, half],
        )
        for p in range(2)
        for half in range(2)
    ]
    for copy in copies:
        copy.start()
    first.wait()
    offs_ref[...] = slots[...].T
    for copy in copies:
        copy.wait()


def pieces(slc, offsets):
    tiles = slc.reshape(2, 16, 8, 2, 2, 128).transpose(0, 1, 3, 4, 2, 5)
    return pl.pallas_call(
        pieces_kernel,
        out_shape=(
            pltpu.VMEM((16, 2, 2, 2, 8, 128), jnp.float32),
            pltpu.VMEM((DATES, SLOTS), jnp.int32),
        ),
        in_specs=[ANY, ANY],
        out_specs=(VMEM, VMEM),
        scratch_shapes=[
            pltpu.VMEM((SLOTS, DATES), jnp.int32),
            pltpu.SemaphoreType.DMA((2, 2)),
            pltpu.SemaphoreType.DMA,
        ],
        name="pieces",
    )(tiles, offsets.T)


def edge_kernel(offs_ref, tiles_ref, edge_ref, shifted, stack):
    half = own_half()
    lanes = lax.broadcasted_iota(jnp.int32, (DATES, 128), 1)
    packed = []
    for p in range(2):
        value = jnp.zeros((DATES, 128), jnp.float32)
        for i in range(8):
            row = tiles_ref[pl.ds(16 * p + 8 * half + i, DATES, stride=32), :]
            value = jnp.where(lanes // 16 == i, pltpu.roll(row, 16 * (half + i), 1), value)
        packed.append(value)
    packed.append(packed[0] * packed[0] + packed[1] * packed[1])
    for q in range(3):
        shifted[q, 0:DATES, :] = packed[q]
        shifted[q, DATES : DATES + 8, :] = jnp.zeros((8, 128), jnp.float32)
    offs = offs_ref[...]
    looks = [None] * (MAPS - 1) + [packed[2]]
    for j in range(SLOTS):
        offset = jnp.broadcast_to(offs[:, j : j + 1], (DATES, 128))
        partner = [jnp.zeros((DATES, 128), jnp.float32)] * 3
        for step in range(1, MAX_OFFSET + 1):
            partner = [jnp.where(offset == step, shifted[q, step : step + DATES, :], partner[q]) for q in range(3)]
        looks[j] = packed[0] * partner[0] + packed[1] * partner[1]
        looks[SLOTS + j] = packed[1] * partner[0] - packed[0] * partner[1]
        looks[2 * SLOTS + j] = partner[2]
    for m in range(MAPS):
        for q, part in enumerate(two_parts(looks[m] / 64.0)):
            stack[DATES * m : DATES * m + DATES, 128 * q : 128 * q + 128] = part
    lane = lax.broadcasted_iota(jnp.int32, (256, 128), 0)
    place = lax.broadcasted_iota(jnp.int32, (256, 128), 1)
    sums = ((lane % 128) // 64 == place % 2).astype(jnp.bfloat16)
    out = jnp.dot(stack[...], sums, preferred_element_type=jnp.float32)
    edge = jnp.zeros((DATES, 128), jnp.float32)
    for m in range(MAPS):
        edge = jnp.where((lanes - HALO_LANE) // 2 == m, out[DATES * m : DATES * m + DATES, :], edge)
    edge_ref[...] = jnp.where(lanes >= HALO_LANE, edge, 0.0)


def edge_looks(offsets, tiles):
    return pl.pallas_call(
        edge_kernel,
        out_shape=pltpu.VMEM((DATES, 128), jnp.float32),
        in_specs=[VMEM, VMEM],
        out_specs=VMEM,
        scratch_shapes=[
            pltpu.VMEM((3, DATES + 8, 128), jnp.float32),
            pltpu.VMEM((MAPS * DATES, 256), jnp.bfloat16),
        ],
        name="edge_looks",
    )(in_vmem(offsets), in_vmem(tiles))


def looks_kernel(offs_smem, offs_ref, tiles_ref, looks_ref, prod, stack):
    def tile(d, p, t):
        return tiles_ref[pl.ds(pl.multiple_of(d * 32 + 16 * p + 8 * t, 8), 8), :]

    def powers(d, carry):
        for t in range(2):
            real, imag = tile(d, 0, t), tile(d, 1, t)
            prod[t, 2 * SLOTS, pl.ds(pl.multiple_of(d * 8, 8), 8), :] = real * real + imag * imag
        return carry

    lax.fori_loop(0, DATES, powers, 0, unroll=4)

    def pairs(d, carry):
        rows = pl.ds(pl.multiple_of(d * 8, 8), 8)
        for t in range(2):
            master_real, master_imag = tile(d, 0, t), tile(d, 1, t)
            for j in range(SLOTS):
                p = jnp.minimum(d + offs_smem[d, j], DATES - 1)
                partner_real, partner_imag = tile(p, 0, t), tile(p, 1, t)
                prod[t, j, rows, :] = master_real * partner_real + master_imag * partner_imag
                prod[t, SLOTS + j, rows, :] = master_imag * partner_real - master_real * partner_imag
        return carry

    lax.fori_loop(0, DATES, pairs, 0, unroll=2)

    offs = offs_ref[...]
    live = (offs > 0).astype(jnp.float32) / 64.0
    lives = [jnp.broadcast_to(live[:, j : j + 1], (DATES, 128)) for j in range(SLOTS)]
    for m in range(2 * SLOTS + 1):
        scale = lives[m % SLOTS] if m < 2 * SLOTS else 1.0 / 64.0
        for r in range(2):
            g = 2 * m + r
            for t in range(2):
                total = prod[t, m, pl.ds(4 * r, DATES, stride=8), :]
                for i in range(1, 4):
                    total = total + prod[t, m, pl.ds(4 * r + i, DATES, stride=8), :]
                for q, part in enumerate(two_parts(total * scale)):
                    lanes = 128 * (2 * t + q)
                    stack[pl.ds(DATES * g, DATES), lanes : lanes + 128] = part

    lane = lax.broadcasted_iota(jnp.int32, (512, 128), 0)
    place = lax.broadcasted_iota(jnp.int32, (512, 128), 1)
    sums = ((lane // 256) * 8 + (lane % 128) // 16 == place % 16).astype(jnp.bfloat16)
    out = jnp.dot(stack[...], sums, preferred_element_type=jnp.float32)
    found = [out[DATES * g : DATES * g + DATES, :] for g in range(4 * SLOTS + 2)]

    column = lax.broadcasted_iota(jnp.int32, (DATES, 2 * DATES), 1) % DATES
    date = lax.broadcasted_iota(jnp.int32, (DATES, 2 * DATES), 0)
    pick = []
    for j in range(SLOTS):
        offset = jnp.broadcast_to(offs[:, j : j + 1], (DATES, 2 * DATES))
        pick.append(((column == date + offset) & (offset > 0)).astype(jnp.float32))
    own = [jnp.concatenate(two_parts(value), axis=0) for value in found[4 * SLOTS :]]
    partner = jnp.dot(
        jnp.concatenate(pick, axis=0).astype(jnp.bfloat16),
        jnp.concatenate(own, axis=1),
        preferred_element_type=jnp.float32,
    )
    picked = [
        partner[DATES * j : DATES * j + DATES, 128 * r : 128 * r + 128] for j in range(SLOTS) for r in range(2)
    ]
    found = found[: 4 * SLOTS] + picked + found[4 * SLOTS :]

    lanes = lax.broadcasted_iota(jnp.int32, (DATES, 128), 1)
    for k in range(4):
        block = jnp.zeros((DATES, 128), jnp.float32)
        for g in range(8 * k, min(8 * k + 8, GROUPS)):
            block = jnp.where(lanes // 16 == g - 8 * k, found[g], block)
        looks_ref[pl.ds(k, DATES, stride=4), :] = block


def local_looks(offsets, tiles):
    return pl.pallas_call(
        looks_kernel,
        out_shape=pltpu.VMEM((4 * DATES, 128), jnp.float32),
        in_specs=[pl.BlockSpec(memory_space=pltpu.SMEM), VMEM, VMEM],
        out_specs=VMEM,
        scratch_shapes=[
            pltpu.VMEM((2, 2 * SLOTS + 1, 8 * DATES, 128), jnp.float32),
            pltpu.VMEM(((4 * SLOTS + 2) * DATES, 512), jnp.bfloat16),
        ],
        name="looks",
    )(offsets, in_vmem(offsets), in_vmem(tiles))


def with_edge_kernel(looks_ref, edge_ref, out_ref):
    rows = pl.ds(3, DATES, stride=4)
    out_ref[rows, :] = looks_ref[rows, :] + edge_ref[...]


def with_edge(looks, edge):
    return pl.pallas_call(
        with_edge_kernel,
        out_shape=pltpu.VMEM((4 * DATES, 128), jnp.float32),
        in_specs=[VMEM, VMEM],
        out_specs=VMEM,
        input_output_aliases={0: 0},
        name="with_edge",
    )(in_vmem(looks), in_vmem(edge))


def finish_kernel(offs_ref, looks_ref, inter_out, coh_out, inter_ref, coh_ref, sems):
    odd = odd_col()
    lanes = lax.broadcasted_iota(jnp.int32, (16, 128), 1)
    blocks = [
        [looks_ref[pl.ds(4 * jnp.bitwise_xor(odd, half) + k, 16, stride=8), :] for k in range(4)]
        for half in range(2)
    ]

    def cells(m, r):
        g = 2 * m + r
        k, at = g // 8, 16 * (g % 8)
        value = jnp.zeros((16, 128), jnp.float32)
        for half in range(2):
            piece = pltpu.roll(blocks[half][k], (16 * half - at) % 128, 1)
            value = jnp.where(lanes // 16 == half, piece, value)
        left = pltpu.roll(blocks[0][3], (127 - HALO_LANE - g) % 128, 1)
        right = pltpu.roll(blocks[1][3], (32 - HALO_LANE - g) % 128, 1)
        return jnp.where(lanes == 127, left, jnp.where(lanes == 32, right, value))

    row = lax.broadcasted_iota(jnp.int32, (16, 128), 0)

    def window(m):
        across = []
        for r in range(2):
            value = cells(m, r)
            if m < 2 * SLOTS:
                inter_ref[m // SLOTS, 0, m % SLOTS, pl.ds(r, 16, stride=2), :] = value[:, :32]
            across.append(value + pltpu.roll(value, 1, 1) + pltpu.roll(value, 127, 1))
        both = across[0] + across[1]
        above = jnp.where(row == 0, 0.0, pltpu.roll(across[1], 1, 0))
        below = jnp.where(row == 15, 0.0, pltpu.roll(across[0], 15, 0))
        return both + above, both + below

    copies = []
    own = window(MAPS - 1)
    lives = (offs_ref[pl.ds(lax.axis_index("date"), 1), :] > 0).astype(jnp.float32)
    for j in range(SLOTS):
        live = jnp.broadcast_to(lives[:, j : j + 1], (16, 128))
        real, imag = window(j), window(SLOTS + j)
        for p in range(2):
            copy = pltpu.make_async_copy(inter_ref.at[p, 0, j], inter_out.at[p, 0, j], sems.at[p, j])
            copy.start()
            copies.append(copy)
        partner = window(2 * SLOTS + j)
        for r in range(2):
            magnitude = jnp.sqrt(real[r] * real[r] + imag[r] * imag[r])
            value = magnitude / (jnp.sqrt((own[r] * live) * partner[r]) + epsilon)
            coh_ref[0, j, pl.ds(r, 16, stride=2), :] = value[:, :32]
        last = pltpu.make_async_copy(coh_ref.at[0, j], coh_out.at[0, j], sems.at[2, j])
        last.start()
        copies.append(last)
    for copy in copies:
        copy.wait()


def finish(offsets, looks):
    return pl.pallas_call(
        finish_kernel,
        out_shape=(
            jax.ShapeDtypeStruct((2, 1, SLOTS, 32, 32), jnp.float32),
            jax.ShapeDtypeStruct((1, SLOTS, 32, 32), jnp.float32),
        ),
        in_specs=[VMEM, VMEM],
        out_specs=(ANY, ANY),
        scratch_shapes=[
            pltpu.VMEM((2, 1, SLOTS, 32, 32), jnp.float32),
            pltpu.VMEM((1, SLOTS, 32, 32), jnp.float32),
            pltpu.SemaphoreType.DMA((3, SLOTS)),
        ],
        name="finish",
    )(in_vmem(offsets), in_vmem(looks))


def edge_pairs(dates, cols):
    pairs = []
    for c in range(1, cols):
        for d in range(c % 2, dates, 2):
            here, there = d * cols + c, d * cols + c - 1
            pairs += [(here, there), (there, here)]
    return pairs


def shards(slc, offsets):
    tiles, offsets = pieces(slc, offsets)
    tiles = lax.all_to_all(tiles.reshape(DATES, 32, 128), "date", 0, 0, tiled=True)
    tiles = tiles.reshape(32 * DATES, 128)
    edge = edge_looks(offsets, tiles)
    edge = lax.ppermute(edge, ("date", "col"), edge_pairs(DATES, lax.axis_size("col")))
    looks = with_edge(local_looks(offsets, tiles), edge)
    looks = lax.all_to_all(looks.reshape(DATES, 4, 128), "date", 0, 0, tiled=True)
    return finish(offsets, looks.reshape(4 * DATES, 128))


def solution(mesh):
    placed = (P(None, "date", None, "col"), P())
    return jax.shard_map(
        shards,
        mesh=mesh,
        in_specs=placed,
        out_specs=(P(None, "date", None, None, "col"), P("date", None, None, "col")),
        check_vma=False,
    )
```

```python
import jax
import jax.numpy as jnp
from jax import lax
from jax.experimental import pallas as pl
from jax.experimental.pallas import tpu as pltpu
from jax.sharding import PartitionSpec as P

SLOTS = 4
DATES = 32
MAX_OFFSET = 6
MAPS = 3 * SLOTS + 1
GROUPS = 2 * MAPS
HALO_LANE = 32

epsilon = 1e-06

VMEM = pl.BlockSpec(memory_space=pltpu.VMEM)
ANY = pl.BlockSpec(memory_space=pl.ANY)


def in_vmem(value):
    return pltpu.with_memory_space_constraint(value, pltpu.VMEM)


def odd_col():
    return lax.rem(lax.axis_index("col"), 2)


def own_half():
    return lax.rem(lax.axis_index("date") + lax.axis_index("col"), 2)


def two_parts(value):
    high = value.astype(jnp.bfloat16)
    return high, (value - high.astype(jnp.float32)).astype(jnp.bfloat16)


def pieces_kernel(slc_ref, slots_ref, out_ref, offs_ref, slots, sems, slots_sem):
    odd = odd_col()
    first = pltpu.make_async_copy(slots_ref, slots, slots_sem)
    first.start()
    copies = [
        pltpu.make_async_copy(
            slc_ref.at[p, :, half],
            out_ref.at[:, jnp.bitwise_xor(odd, half), p],
            sems.at[p, half],
        )
        for p in range(2)
        for half in range(2)
    ]
    for copy in copies:
        copy.start()
    first.wait()
    offs_ref[...] = slots[...].T
    for copy in copies:
        copy.wait()


def pieces(slc, offsets):
    tiles = slc.reshape(2, 16, 8, 2, 2, 128).transpose(0, 1, 3, 4, 2, 5)
    return pl.pallas_call(
        pieces_kernel,
        out_shape=(
            pltpu.VMEM((16, 2, 2, 2, 8, 128), jnp.float32),
            pltpu.VMEM((DATES, SLOTS), jnp.int32),
        ),
        in_specs=[ANY, ANY],
        out_specs=(VMEM, VMEM),
        scratch_shapes=[
            pltpu.VMEM((SLOTS, DATES), jnp.int32),
            pltpu.SemaphoreType.DMA((2, 2)),
            pltpu.SemaphoreType.DMA,
        ],
        name="pieces",
    )(tiles, offsets.T)


def edge_kernel(offs_ref, tiles_ref, edge_ref, tiles, shifted, stack):
    half = own_half()
    lanes = lax.broadcasted_iota(jnp.int32, (DATES, 128), 1)
    packed = []
    for p in range(2):
        for d in range(DATES):
            tile = tiles_ref[pl.ds(pl.multiple_of(32 * d + 16 * p + 8 * half, 8), 8), :]
            tiles[p, 8 * d : 8 * d + 8, :] = tile
        value = jnp.zeros((DATES, 128), jnp.float32)
        for i in range(8):
            row = tiles[p, pl.ds(i, DATES, stride=8), :]
            value = jnp.where(lanes // 16 == i, pltpu.roll(row, 16 * (half + i), 1), value)
        packed.append(value)
    for p in range(2):
        shifted[p, 0:DATES, :] = packed[p]
        shifted[p, DATES : DATES + 8, :] = jnp.zeros((8, 128), jnp.float32)
    offs = offs_ref[...]
    for top in range(0, DATES, 16):
        rows = slice(top, top + 16)
        real, imag = packed[0][rows, :], packed[1][rows, :]
        offset = [jnp.broadcast_to(offs[rows, j : j + 1], (16, 128)) for j in range(SLOTS)]
        partner = [[jnp.zeros((16, 128), jnp.float32)] * 2 for j in range(SLOTS)]
        for step in range(1, MAX_OFFSET + 1):
            later = [shifted[p, top + step : top + step + 16, :] for p in range(2)]
            for j in range(SLOTS):
                here = offset[j] == step
                partner[j] = [jnp.where(here, later[p], partner[j][p]) for p in range(2)]
        looks = [real * b[0] + imag * b[1] for b in partner]
        looks += [imag * b[0] - real * b[1] for b in partner]
        looks += [b[0] * b[0] + b[1] * b[1] for b in partner]
        looks += [real * real + imag * imag]
        for m in range(MAPS):
            for q, part in enumerate(two_parts(looks[m] / 64.0)):
                stack[DATES * m + top : DATES * m + top + 16, 128 * q : 128 * q + 128] = part
    lane = lax.broadcasted_iota(jnp.int32, (128, 128), 0)
    place = lax.broadcasted_iota(jnp.int32, (128, 128), 1)
    sums = (lane // 64 == place % 2).astype(jnp.bfloat16)
    sums = jnp.concatenate([sums, sums], axis=0)
    out = jnp.dot(stack[...], sums, preferred_element_type=jnp.float32)
    edge = jnp.zeros((DATES, 128), jnp.float32)
    for m in range(MAPS):
        edge = jnp.where((lanes - HALO_LANE) // 2 == m, out[DATES * m : DATES * m + DATES, :], edge)
    edge_ref[...] = jnp.where(lanes >= HALO_LANE, edge, 0.0)


def edge_looks(offsets, tiles):
    return pl.pallas_call(
        edge_kernel,
        out_shape=pltpu.VMEM((DATES, 128), jnp.float32),
        in_specs=[VMEM, VMEM],
        out_specs=VMEM,
        scratch_shapes=[
            pltpu.VMEM((2, 8 * DATES, 128), jnp.float32),
            pltpu.VMEM((2, DATES + 8, 128), jnp.float32),
            pltpu.VMEM((MAPS * DATES, 256), jnp.bfloat16),
        ],
        name="edge_looks",
    )(in_vmem(offsets), in_vmem(tiles))


def looks_kernel(offs_smem, offs_ref, tiles_ref, looks_ref, prod, stack):
    def tile(d, p, t):
        return tiles_ref[pl.ds(pl.multiple_of(d * 32 + 16 * p + 8 * t, 8), 8), :]

    def powers(d, carry):
        for t in range(2):
            real, imag = tile(d, 0, t), tile(d, 1, t)
            prod[t, 2 * SLOTS, pl.ds(pl.multiple_of(d * 8, 8), 8), :] = real * real + imag * imag
        return carry

    lax.fori_loop(0, DATES, powers, 0, unroll=4)

    def pairs(d, carry):
        rows = pl.ds(pl.multiple_of(d * 8, 8), 8)
        for t in range(2):
            master_real, master_imag = tile(d, 0, t), tile(d, 1, t)
            for j in range(SLOTS):
                p = jnp.minimum(d + offs_smem[d, j], DATES - 1)
                partner_real, partner_imag = tile(p, 0, t), tile(p, 1, t)
                prod[t, j, rows, :] = master_real * partner_real + master_imag * partner_imag
                prod[t, SLOTS + j, rows, :] = master_imag * partner_real - master_real * partner_imag
        return carry

    lax.fori_loop(0, DATES, pairs, 0, unroll=2)

    offs = offs_ref[...]
    live = (offs > 0).astype(jnp.float32) / 64.0
    lives = [jnp.broadcast_to(live[:, j : j + 1], (DATES, 128)) for j in range(SLOTS)]
    for m in range(2 * SLOTS + 1):
        scale = lives[m % SLOTS] if m < 2 * SLOTS else 1.0 / 64.0
        for r in range(2):
            g = 2 * m + r
            for t in range(2):
                total = prod[t, m, pl.ds(4 * r, DATES, stride=8), :]
                for i in range(1, 4):
                    total = total + prod[t, m, pl.ds(4 * r + i, DATES, stride=8), :]
                for q, part in enumerate(two_parts(total * scale)):
                    lanes = 128 * (2 * t + q)
                    stack[pl.ds(DATES * g, DATES), lanes : lanes + 128] = part

    lane = lax.broadcasted_iota(jnp.int32, (512, 128), 0)
    place = lax.broadcasted_iota(jnp.int32, (512, 128), 1)
    sums = ((lane // 256) * 8 + (lane % 128) // 16 == place % 16).astype(jnp.bfloat16)
    out = jnp.dot(stack[...], sums, preferred_element_type=jnp.float32)
    found = [out[DATES * g : DATES * g + DATES, :] for g in range(4 * SLOTS + 2)]

    column = lax.broadcasted_iota(jnp.int32, (DATES, 2 * DATES), 1) % DATES
    date = lax.broadcasted_iota(jnp.int32, (DATES, 2 * DATES), 0)
    pick = []
    for j in range(SLOTS):
        offset = jnp.broadcast_to(offs[:, j : j + 1], (DATES, 2 * DATES))
        pick.append(((column == date + offset) & (offset > 0)).astype(jnp.float32))
    own = [jnp.concatenate(two_parts(value), axis=0) for value in found[4 * SLOTS :]]
    partner = jnp.dot(
        jnp.concatenate(pick, axis=0).astype(jnp.bfloat16),
        jnp.concatenate(own, axis=1),
        preferred_element_type=jnp.float32,
    )
    picked = [
        partner[DATES * j : DATES * j + DATES, 128 * r : 128 * r + 128] for j in range(SLOTS) for r in range(2)
    ]
    found = found[: 4 * SLOTS] + picked + found[4 * SLOTS :]

    lanes = lax.broadcasted_iota(jnp.int32, (DATES, 128), 1)
    for k in range(4):
        block = jnp.zeros((DATES, 128), jnp.float32)
        for g in range(8 * k, min(8 * k + 8, GROUPS)):
            block = jnp.where(lanes // 16 == g - 8 * k, found[g], block)
        looks_ref[pl.ds(k, DATES, stride=4), :] = block


def local_looks(offsets, tiles):
    return pl.pallas_call(
        looks_kernel,
        out_shape=pltpu.VMEM((4 * DATES, 128), jnp.float32),
        in_specs=[pl.BlockSpec(memory_space=pltpu.SMEM), VMEM, VMEM],
        out_specs=VMEM,
        scratch_shapes=[
            pltpu.VMEM((2, 2 * SLOTS + 1, 8 * DATES, 128), jnp.float32),
            pltpu.VMEM(((4 * SLOTS + 2) * DATES, 512), jnp.bfloat16),
        ],
        name="looks",
    )(offsets, in_vmem(offsets), in_vmem(tiles))


def with_edge_kernel(looks_ref, edge_ref, out_ref):
    rows = pl.ds(3, DATES, stride=4)
    out_ref[rows, :] = looks_ref[rows, :] + edge_ref[...]


def with_edge(looks, edge):
    return pl.pallas_call(
        with_edge_kernel,
        out_shape=pltpu.VMEM((4 * DATES, 128), jnp.float32),
        in_specs=[VMEM, VMEM],
        out_specs=VMEM,
        input_output_aliases={0: 0},
        name="with_edge",
    )(in_vmem(looks), in_vmem(edge))


def finish_kernel(offs_ref, looks_ref, inter_out, coh_out, inter_ref, coh_ref, sems):
    odd = odd_col()
    lanes = lax.broadcasted_iota(jnp.int32, (16, 128), 1)
    blocks = [
        [looks_ref[pl.ds(4 * jnp.bitwise_xor(odd, half) + k, 16, stride=8), :] for k in range(4)]
        for half in range(2)
    ]

    second = [pltpu.roll(block, 16, 1) for block in blocks[1]]
    halos = jnp.where(lanes < HALO_LANE + 32, blocks[0][3], pltpu.roll(blocks[1][3], 33, 1))

    def cells(m, r):
        g = 2 * m + r
        k, at = g // 8, 16 * (g % 8)
        both = jnp.where(lanes // 16 == g % 8, blocks[0][k], second[k])
        halo = pltpu.roll(halos, (127 - HALO_LANE - g) % 128, 1)
        return jnp.where(lanes < 32, pltpu.roll(both, (128 - at) % 128, 1), halo)

    row = lax.broadcasted_iota(jnp.int32, (16, 128), 0)

    def window(m):
        across = []
        for r in range(2):
            value = cells(m, r)
            if m < 2 * SLOTS:
                inter_ref[m // SLOTS, 0, m % SLOTS, pl.ds(r, 16, stride=2), :] = value[:, :32]
            across.append(value + pltpu.roll(value, 1, 1) + pltpu.roll(value, 127, 1))
        both = across[0] + across[1]
        above = jnp.where(row == 0, 0.0, pltpu.roll(across[1], 1, 0))
        below = jnp.where(row == 15, 0.0, pltpu.roll(across[0], 15, 0))
        return both + above, both + below

    copies = []
    own = window(MAPS - 1)
    lives = (offs_ref[pl.ds(lax.axis_index("date"), 1), :] > 0).astype(jnp.float32)
    for j in range(SLOTS):
        live = jnp.broadcast_to(lives[:, j : j + 1], (16, 128))
        real, imag = window(j), window(SLOTS + j)
        for p in range(2):
            copy = pltpu.make_async_copy(inter_ref.at[p, 0, j], inter_out.at[p, 0, j], sems.at[p, j])
            copy.start()
            copies.append(copy)
        partner = window(2 * SLOTS + j)
        for r in range(2):
            magnitude = jnp.sqrt(real[r] * real[r] + imag[r] * imag[r])
            value = magnitude / (jnp.sqrt((own[r] * live) * partner[r]) + epsilon)
            coh_ref[0, j, pl.ds(r, 16, stride=2), :] = value[:, :32]
        last = pltpu.make_async_copy(coh_ref.at[0, j], coh_out.at[0, j], sems.at[2, j])
        last.start()
        copies.append(last)
    for copy in copies:
        copy.wait()


def finish(offsets, looks):
    return pl.pallas_call(
        finish_kernel,
        out_shape=(
            jax.ShapeDtypeStruct((2, 1, SLOTS, 32, 32), jnp.float32),
            jax.ShapeDtypeStruct((1, SLOTS, 32, 32), jnp.float32),
        ),
        in_specs=[VMEM, VMEM],
        out_specs=(ANY, ANY),
        scratch_shapes=[
            pltpu.VMEM((2, 1, SLOTS, 32, 32), jnp.float32),
            pltpu.VMEM((1, SLOTS, 32, 32), jnp.float32),
            pltpu.SemaphoreType.DMA((3, SLOTS)),
        ],
        name="finish",
    )(in_vmem(offsets), in_vmem(looks))


def edge_pairs(dates, cols):
    pairs = []
    for c in range(1, cols):
        for d in range(c % 2, dates, 2):
            here, there = d * cols + c, d * cols + c - 1
            pairs += [(here, there), (there, here)]
    return pairs


def shards(slc, offsets):
    tiles, offsets = pieces(slc, offsets)
    tiles = lax.all_to_all(tiles.reshape(DATES, 32, 128), "date", 0, 0, tiled=True)
    tiles = tiles.reshape(32 * DATES, 128)
    edge = edge_looks(offsets, tiles)
    edge = lax.ppermute(edge, ("date", "col"), edge_pairs(DATES, lax.axis_size("col")))
    looks = with_edge(local_looks(offsets, tiles), edge)
    looks = lax.all_to_all(looks.reshape(DATES, 4, 128), "date", 0, 0, tiled=True)
    return finish(offsets, looks.reshape(4 * DATES, 128))


def solution(mesh):
    placed = (P(None, "date", None, "col"), P())
    return jax.shard_map(
        shards,
        mesh=mesh,
        in_specs=placed,
        out_specs=(P(None, "date", None, None, "col"), P("date", None, None, "col")),
        check_vma=False,
    )
```

```python
import jax
import jax.numpy as jnp
from jax import lax
from jax.experimental import pallas as pl
from jax.experimental.pallas import tpu as pltpu
from jax.sharding import PartitionSpec as P

SLOTS = 4
DATES = 32
MAX_OFFSET = 6
MAPS = 3 * SLOTS + 1
GROUPS = 2 * MAPS
HALO_LANE = 32

epsilon = 1e-06

VMEM = pl.BlockSpec(memory_space=pltpu.VMEM)
ANY = pl.BlockSpec(memory_space=pl.ANY)


def in_vmem(value):
    return pltpu.with_memory_space_constraint(value, pltpu.VMEM)


def odd_col():
    return lax.rem(lax.axis_index("col"), 2)


def own_half():
    return lax.rem(lax.axis_index("date") + lax.axis_index("col"), 2)


def two_parts(value):
    high = value.astype(jnp.bfloat16)
    return high, (value - high.astype(jnp.float32)).astype(jnp.bfloat16)


def pieces_kernel(slc_ref, slots_ref, out_ref, offs_ref, planes, slots, sems, slots_sem):
    odd = odd_col()
    first = pltpu.make_async_copy(slots_ref, slots, slots_sem)
    first.start()
    copies = [pltpu.make_async_copy(slc_ref.at[p], planes.at[p], sems.at[p]) for p in range(2)]
    for copy in copies:
        copy.start()
    first.wait()
    offs_ref[...] = slots[...].T
    for p, copy in enumerate(copies):
        copy.wait()
        for block in range(16):
            for half in range(2):
                out_ref[block, jnp.bitwise_xor(odd, half), p] = planes[p, block, half]


def pieces(slc, offsets):
    tiles = slc.reshape(2, 16, 8, 2, 2, 128).transpose(0, 1, 3, 4, 2, 5)
    return pl.pallas_call(
        pieces_kernel,
        out_shape=(
            pltpu.VMEM((16, 2, 2, 2, 8, 128), jnp.float32),
            pltpu.VMEM((DATES, SLOTS), jnp.int32),
        ),
        in_specs=[ANY, ANY],
        out_specs=(VMEM, VMEM),
        scratch_shapes=[
            pltpu.VMEM((2, 16, 2, 2, 8, 128), jnp.float32),
            pltpu.VMEM((SLOTS, DATES), jnp.int32),
            pltpu.SemaphoreType.DMA((2,)),
            pltpu.SemaphoreType.DMA,
        ],
        name="pieces",
    )(tiles, offsets.T)


def edge_kernel(offs_ref, tiles_ref, edge_ref, tiles, shifted, stack):
    half = own_half()
    lanes = lax.broadcasted_iota(jnp.int32, (DATES, 128), 1)
    packed = []
    for p in range(2):
        for d in range(DATES):
            tile = tiles_ref[pl.ds(pl.multiple_of(32 * d + 16 * p + 8 * half, 8), 8), :]
            tiles[p, 8 * d : 8 * d + 8, :] = tile
        value = jnp.zeros((DATES, 128), jnp.float32)
        for i in range(8):
            row = tiles[p, pl.ds(i, DATES, stride=8), :]
            value = jnp.where(lanes // 16 == i, pltpu.roll(row, 16 * (half + i), 1), value)
        packed.append(value)
    for p in range(2):
        shifted[p, 0:DATES, :] = packed[p]
        shifted[p, DATES : DATES + 8, :] = jnp.zeros((8, 128), jnp.float32)
    offs = offs_ref[...]
    for top in range(0, DATES, 16):
        rows = slice(top, top + 16)
        real, imag = packed[0][rows, :], packed[1][rows, :]
        offset = [jnp.broadcast_to(offs[rows, j : j + 1], (16, 128)) for j in range(SLOTS)]
        partner = [[jnp.zeros((16, 128), jnp.float32)] * 2 for j in range(SLOTS)]
        for step in range(1, MAX_OFFSET + 1):
            later = [shifted[p, top + step : top + step + 16, :] for p in range(2)]
            for j in range(SLOTS):
                here = offset[j] == step
                partner[j] = [jnp.where(here, later[p], partner[j][p]) for p in range(2)]
        looks = [real * b[0] + imag * b[1] for b in partner]
        looks += [imag * b[0] - real * b[1] for b in partner]
        looks += [b[0] * b[0] + b[1] * b[1] for b in partner]
        looks += [real * real + imag * imag]
        for m in range(MAPS):
            for q, part in enumerate(two_parts(looks[m])):
                stack[DATES * m + top : DATES * m + top + 16, 128 * q : 128 * q + 128] = part
    lane = lax.broadcasted_iota(jnp.int32, (128, 128), 0)
    place = lax.broadcasted_iota(jnp.int32, (128, 128), 1)
    sums = jnp.where(lane // 64 == place % 2, 1.0 / 64.0, 0.0).astype(jnp.bfloat16)
    sums = jnp.concatenate([sums, sums], axis=0)
    out = jnp.dot(stack[...], sums, preferred_element_type=jnp.float32)
    lanes = lax.broadcasted_iota(jnp.int32, (8, 128), 1)
    block = jnp.zeros((8, 128), jnp.float32)
    for x in range(4):
        for m in range(MAPS):
            at = DATES * m + 8 * x
            block = jnp.where(lanes // 2 == 16 * x + m, out[at : at + 8, :], block)
    edge_ref[...] = block


def edge_looks(offsets, tiles):
    return pl.pallas_call(
        edge_kernel,
        out_shape=pltpu.VMEM((8, 128), jnp.float32),
        in_specs=[VMEM, VMEM],
        out_specs=VMEM,
        scratch_shapes=[
            pltpu.VMEM((2, 8 * DATES, 128), jnp.float32),
            pltpu.VMEM((2, DATES + 8, 128), jnp.float32),
            pltpu.VMEM((MAPS * DATES, 256), jnp.bfloat16),
        ],
        name="edge_looks",
    )(in_vmem(offsets), in_vmem(tiles))


def looks_kernel(offs_smem, offs_ref, tiles_ref, looks_ref, prod, stack):
    def tile(d, p, t):
        return tiles_ref[pl.ds(pl.multiple_of(d * 32 + 16 * p + 8 * t, 8), 8), :]

    def powers(d, carry):
        for t in range(2):
            real, imag = tile(d, 0, t), tile(d, 1, t)
            prod[t, 2 * SLOTS, pl.ds(pl.multiple_of(d * 8, 8), 8), :] = real * real + imag * imag
        return carry

    lax.fori_loop(0, DATES, powers, 0, unroll=4)

    def pairs(d, carry):
        rows = pl.ds(pl.multiple_of(d * 8, 8), 8)
        for t in range(2):
            master_real, master_imag = tile(d, 0, t), tile(d, 1, t)
            for j in range(SLOTS):
                p = jnp.minimum(d + offs_smem[d, j], DATES - 1)
                partner_real, partner_imag = tile(p, 0, t), tile(p, 1, t)
                prod[t, j, rows, :] = master_real * partner_real + master_imag * partner_imag
                prod[t, SLOTS + j, rows, :] = master_imag * partner_real - master_real * partner_imag
        return carry

    lax.fori_loop(0, DATES, pairs, 0, unroll=2)

    offs = offs_ref[...]
    live = (offs > 0).astype(jnp.float32) / 64.0
    lives = [jnp.broadcast_to(live[:, j : j + 1], (DATES, 128)) for j in range(SLOTS)]
    for m in range(2 * SLOTS + 1):
        scale = lives[m % SLOTS] if m < 2 * SLOTS else 1.0 / 64.0
        for r in range(2):
            g = 2 * m + r
            for t in range(2):
                total = prod[t, m, pl.ds(4 * r, DATES, stride=8), :]
                for i in range(1, 4):
                    total = total + prod[t, m, pl.ds(4 * r + i, DATES, stride=8), :]
                for q, part in enumerate(two_parts(total * scale)):
                    lanes = 128 * (2 * t + q)
                    stack[pl.ds(DATES * g, DATES), lanes : lanes + 128] = part

    lane = lax.broadcasted_iota(jnp.int32, (512, 128), 0)
    place = lax.broadcasted_iota(jnp.int32, (512, 128), 1)
    sums = ((lane // 256) * 8 + (lane % 128) // 16 == place % 16).astype(jnp.bfloat16)
    out = jnp.dot(stack[...], sums, preferred_element_type=jnp.float32)
    found = [out[DATES * g : DATES * g + DATES, :] for g in range(4 * SLOTS + 2)]

    column = lax.broadcasted_iota(jnp.int32, (DATES, 2 * DATES), 1) % DATES
    date = lax.broadcasted_iota(jnp.int32, (DATES, 2 * DATES), 0)
    pick = []
    for j in range(SLOTS):
        offset = jnp.broadcast_to(offs[:, j : j + 1], (DATES, 2 * DATES))
        pick.append(((column == date + offset) & (offset > 0)).astype(jnp.float32))
    own = [jnp.concatenate(two_parts(value), axis=0) for value in found[4 * SLOTS :]]
    partner = jnp.dot(
        jnp.concatenate(pick, axis=0).astype(jnp.bfloat16),
        jnp.concatenate(own, axis=1),
        preferred_element_type=jnp.float32,
    )
    picked = [
        partner[DATES * j : DATES * j + DATES, 128 * r : 128 * r + 128] for j in range(SLOTS) for r in range(2)
    ]
    found = found[: 4 * SLOTS] + picked + found[4 * SLOTS :]

    lanes = lax.broadcasted_iota(jnp.int32, (DATES, 128), 1)
    for k in range(4):
        block = jnp.zeros((DATES, 128), jnp.float32)
        for g in range(8 * k, min(8 * k + 8, GROUPS)):
            block = jnp.where(lanes // 16 == g - 8 * k, found[g], block)
        looks_ref[pl.ds(k, DATES, stride=4), :] = block


def local_looks(offsets, tiles):
    return pl.pallas_call(
        looks_kernel,
        out_shape=pltpu.VMEM((4 * DATES, 128), jnp.float32),
        in_specs=[pl.BlockSpec(memory_space=pltpu.SMEM), VMEM, VMEM],
        out_specs=VMEM,
        scratch_shapes=[
            pltpu.VMEM((2, 2 * SLOTS + 1, 8 * DATES, 128), jnp.float32),
            pltpu.VMEM(((4 * SLOTS + 2) * DATES, 512), jnp.bfloat16),
        ],
        name="looks",
    )(offsets, in_vmem(offsets), in_vmem(tiles))


def with_edge_kernel(looks_ref, edge_ref, out_ref):
    edge = edge_ref[...]
    lanes = lax.broadcasted_iota(jnp.int32, (8, 128), 1)
    for x in range(4):
        rows = pl.ds(DATES * x + 3, 8, stride=4)
        piece = pltpu.roll(edge, (HALO_LANE - 32 * x) % 128, 1)
        out_ref[rows, :] = jnp.where(lanes // 32 == HALO_LANE // 32, piece, looks_ref[rows, :])


def with_edge(looks, edge):
    return pl.pallas_call(
        with_edge_kernel,
        out_shape=pltpu.VMEM((4 * DATES, 128), jnp.float32),
        in_specs=[VMEM, VMEM],
        out_specs=VMEM,
        input_output_aliases={0: 0},
        name="with_edge",
    )(in_vmem(looks), in_vmem(edge))


def finish_kernel(offs_ref, looks_ref, inter_out, coh_out, inter_ref, coh_ref, sems):
    odd = odd_col()
    lanes = lax.broadcasted_iota(jnp.int32, (16, 128), 1)
    blocks = [
        [looks_ref[pl.ds(4 * jnp.bitwise_xor(odd, half) + k, 16, stride=8), :] for k in range(4)]
        for half in range(2)
    ]

    second = [pltpu.roll(block, 16, 1) for block in blocks[1]]
    halos = jnp.where(lanes < HALO_LANE + 32, blocks[0][3], pltpu.roll(blocks[1][3], 33, 1))

    def cells(m, r):
        g = 2 * m + r
        k, at = g // 8, 16 * (g % 8)
        both = jnp.where(lanes // 16 == g % 8, blocks[0][k], second[k])
        halo = pltpu.roll(halos, (127 - HALO_LANE - g) % 128, 1)
        return jnp.where(lanes < 32, pltpu.roll(both, (128 - at) % 128, 1), halo)

    row = lax.broadcasted_iota(jnp.int32, (16, 128), 0)

    def window(m):
        across = []
        for r in range(2):
            value = cells(m, r)
            if m < 2 * SLOTS:
                inter_ref[m // SLOTS, 0, m % SLOTS, pl.ds(r, 16, stride=2), :] = value[:, :32]
            across.append(value + pltpu.roll(value, 1, 1) + pltpu.roll(value, 127, 1))
        both = across[0] + across[1]
        above = jnp.where(row == 0, 0.0, pltpu.roll(across[1], 1, 0))
        below = jnp.where(row == 15, 0.0, pltpu.roll(across[0], 15, 0))
        return both + above, both + below

    copies = []
    own = window(MAPS - 1)
    lives = (offs_ref[pl.ds(lax.axis_index("date"), 1), :] > 0).astype(jnp.float32)
    for j in range(SLOTS):
        live = jnp.broadcast_to(lives[:, j : j + 1], (16, 128))
        real, imag = window(j), window(SLOTS + j)
        for p in range(2):
            copy = pltpu.make_async_copy(inter_ref.at[p, 0, j], inter_out.at[p, 0, j], sems.at[p, j])
            copy.start()
            copies.append(copy)
        partner = window(2 * SLOTS + j)
        for r in range(2):
            magnitude = jnp.sqrt(real[r] * real[r] + imag[r] * imag[r])
            value = magnitude / (jnp.sqrt((own[r] * live) * partner[r]) + epsilon)
            coh_ref[0, j, pl.ds(r, 16, stride=2), :] = value[:, :32]
        last = pltpu.make_async_copy(coh_ref.at[0, j], coh_out.at[0, j], sems.at[2, j])
        last.start()
        copies.append(last)
    for copy in copies:
        copy.wait()


def finish(offsets, looks):
    return pl.pallas_call(
        finish_kernel,
        out_shape=(
            jax.ShapeDtypeStruct((2, 1, SLOTS, 32, 32), jnp.float32),
            jax.ShapeDtypeStruct((1, SLOTS, 32, 32), jnp.float32),
        ),
        in_specs=[VMEM, VMEM],
        out_specs=(ANY, ANY),
        scratch_shapes=[
            pltpu.VMEM((2, 1, SLOTS, 32, 32), jnp.float32),
            pltpu.VMEM((1, SLOTS, 32, 32), jnp.float32),
            pltpu.SemaphoreType.DMA((3, SLOTS)),
        ],
        name="finish",
    )(in_vmem(offsets), in_vmem(looks))


def edge_pairs(dates, cols):
    pairs = []
    for c in range(1, cols):
        for d in range(c % 2, dates, 2):
            here, there = d * cols + c, d * cols + c - 1
            pairs += [(here, there), (there, here)]
    return pairs


def shards(slc, offsets):
    tiles, offsets = pieces(slc, offsets)
    tiles = lax.all_to_all(tiles.reshape(DATES, 32, 128), "date", 0, 0, tiled=True)
    tiles = tiles.reshape(32 * DATES, 128)
    edge = edge_looks(offsets, tiles)
    edge = lax.ppermute(edge, ("date", "col"), edge_pairs(DATES, lax.axis_size("col")))
    looks = with_edge(local_looks(offsets, tiles), edge)
    looks = lax.all_to_all(looks.reshape(DATES, 4, 128), "date", 0, 0, tiled=True)
    return finish(offsets, looks.reshape(4 * DATES, 128))


def solution(mesh):
    placed = (P(None, "date", None, "col"), P())
    return jax.shard_map(
        shards,
        mesh=mesh,
        in_specs=placed,
        out_specs=(P(None, "date", None, None, "col"), P("date", None, None, "col")),
        check_vma=False,
    )
```

```python
import jax
import jax.numpy as jnp
from jax import lax
from jax.experimental import pallas as pl
from jax.experimental.pallas import tpu as pltpu
from jax.sharding import PartitionSpec as P

SLOTS = 4
DATES = 32
MAX_OFFSET = 6
MAPS = 3 * SLOTS + 1
GROUPS = 2 * MAPS
HALO_LANE = 32

epsilon = 1e-06

VMEM = pl.BlockSpec(memory_space=pltpu.VMEM)
ANY = pl.BlockSpec(memory_space=pl.ANY)


def in_vmem(value):
    return pltpu.with_memory_space_constraint(value, pltpu.VMEM)


def odd_col():
    return lax.rem(lax.axis_index("col"), 2)


def own_half():
    return lax.rem(lax.axis_index("date") + lax.axis_index("col"), 2)


def two_parts(value):
    high = value.astype(jnp.bfloat16)
    return high, (value - high.astype(jnp.float32)).astype(jnp.bfloat16)


def pieces_kernel(slc_ref, slots_ref, out_ref, offs_ref, planes, slots, sems, slots_sem):
    odd = odd_col()
    first = pltpu.make_async_copy(slots_ref, slots, slots_sem)
    first.start()
    copies = [pltpu.make_async_copy(slc_ref.at[p], planes.at[p], sems.at[p]) for p in range(2)]
    for copy in copies:
        copy.start()
    first.wait()
    offs_ref[...] = slots[...].T
    for p, copy in enumerate(copies):
        copy.wait()
        for block in range(16):
            for half in range(2):
                out_ref[block, jnp.bitwise_xor(odd, half), p] = planes[p, block, half]


def pieces(slc, offsets):
    tiles = slc.reshape(2, 16, 8, 2, 2, 128).transpose(0, 1, 3, 4, 2, 5)
    return pl.pallas_call(
        pieces_kernel,
        out_shape=(
            pltpu.VMEM((16, 2, 2, 2, 8, 128), jnp.float32),
            pltpu.VMEM((DATES, SLOTS), jnp.int32),
        ),
        in_specs=[ANY, ANY],
        out_specs=(VMEM, VMEM),
        scratch_shapes=[
            pltpu.VMEM((2, 16, 2, 2, 8, 128), jnp.float32),
            pltpu.VMEM((SLOTS, DATES), jnp.int32),
            pltpu.SemaphoreType.DMA((2,)),
            pltpu.SemaphoreType.DMA,
        ],
        name="pieces",
    )(tiles, offsets.T)


def edge_kernel(offs_ref, tiles_ref, edge_ref, tiles, shifted, stack):
    half = own_half()
    lanes = lax.broadcasted_iota(jnp.int32, (DATES, 128), 1)
    packed = []
    for p in range(2):
        for d in range(DATES):
            tile = tiles_ref[pl.ds(pl.multiple_of(32 * d + 16 * p + 8 * half, 8), 8), :]
            tiles[p, 8 * d : 8 * d + 8, :] = tile
        value = jnp.zeros((DATES, 128), jnp.float32)
        for i in range(8):
            row = tiles[p, pl.ds(i, DATES, stride=8), :]
            value = jnp.where(lanes // 16 == i, pltpu.roll(row, 16 * (half + i), 1), value)
        packed.append(value)
    for p in range(2):
        shifted[p, 0:DATES, :] = packed[p]
        shifted[p, DATES : DATES + 8, :] = jnp.zeros((8, 128), jnp.float32)
    offs = offs_ref[...]
    for top in range(0, DATES, 16):
        rows = slice(top, top + 16)
        real, imag = packed[0][rows, :], packed[1][rows, :]
        offset = [jnp.broadcast_to(offs[rows, j : j + 1], (16, 128)) for j in range(SLOTS)]
        partner = [[jnp.zeros((16, 128), jnp.float32)] * 2 for j in range(SLOTS)]
        for step in range(1, MAX_OFFSET + 1):
            later = [shifted[p, top + step : top + step + 16, :] for p in range(2)]
            for j in range(SLOTS):
                here = offset[j] == step
                partner[j] = [jnp.where(here, later[p], partner[j][p]) for p in range(2)]
        looks = [real * b[0] + imag * b[1] for b in partner]
        looks += [imag * b[0] - real * b[1] for b in partner]
        looks += [b[0] * b[0] + b[1] * b[1] for b in partner]
        looks += [real * real + imag * imag]
        for m in range(MAPS):
            for q, part in enumerate(two_parts(looks[m])):
                stack[DATES * m + top : DATES * m + top + 16, 128 * q : 128 * q + 128] = part
    lane = lax.broadcasted_iota(jnp.int32, (128, 128), 0)
    place = lax.broadcasted_iota(jnp.int32, (128, 128), 1)
    sums = jnp.where(lane // 64 == place % 2, 1.0 / 64.0, 0.0).astype(jnp.bfloat16)
    sums = jnp.concatenate([sums, sums], axis=0)
    out = jnp.dot(stack[...], sums, preferred_element_type=jnp.float32)
    edge = jnp.zeros((DATES, 128), jnp.float32)
    for m in range(MAPS):
        edge = jnp.where((lanes - HALO_LANE) // 2 == m, out[DATES * m : DATES * m + DATES, :], edge)
    edge_ref[...] = jnp.where(lanes >= HALO_LANE, edge, 0.0)


def edge_looks(offsets, tiles):
    return pl.pallas_call(
        edge_kernel,
        out_shape=pltpu.VMEM((DATES, 128), jnp.float32),
        in_specs=[VMEM, VMEM],
        out_specs=VMEM,
        scratch_shapes=[
            pltpu.VMEM((2, 8 * DATES, 128), jnp.float32),
            pltpu.VMEM((2, DATES + 8, 128), jnp.float32),
            pltpu.VMEM((MAPS * DATES, 256), jnp.bfloat16),
        ],
        name="edge_looks",
    )(in_vmem(offsets), in_vmem(tiles))


def looks_kernel(offs_smem, offs_ref, tiles_ref, looks_ref, prod, stack):
    def tile(d, p, t):
        return tiles_ref[pl.ds(pl.multiple_of(d * 32 + 16 * p + 8 * t, 8), 8), :]

    def powers(d, carry):
        for t in range(2):
            real, imag = tile(d, 0, t), tile(d, 1, t)
            prod[t, 2 * SLOTS, pl.ds(pl.multiple_of(d * 8, 8), 8), :] = real * real + imag * imag
        return carry

    lax.fori_loop(0, DATES, powers, 0, unroll=4)

    def pairs(d, carry):
        rows = pl.ds(pl.multiple_of(d * 8, 8), 8)
        for t in range(2):
            master_real, master_imag = tile(d, 0, t), tile(d, 1, t)
            for j in range(SLOTS):
                p = jnp.minimum(d + offs_smem[d, j], DATES - 1)
                partner_real, partner_imag = tile(p, 0, t), tile(p, 1, t)
                prod[t, j, rows, :] = master_real * partner_real + master_imag * partner_imag
                prod[t, SLOTS + j, rows, :] = master_imag * partner_real - master_real * partner_imag
        return carry

    lax.fori_loop(0, DATES, pairs, 0, unroll=2)

    offs = offs_ref[...]
    live = (offs > 0).astype(jnp.float32) / 64.0
    lives = [jnp.broadcast_to(live[:, j : j + 1], (DATES, 128)) for j in range(SLOTS)]
    for m in range(2 * SLOTS + 1):
        scale = lives[m % SLOTS] if m < 2 * SLOTS else 1.0 / 64.0
        for r in range(2):
            g = 2 * m + r
            for t in range(2):
                total = prod[t, m, pl.ds(4 * r, DATES, stride=8), :]
                for i in range(1, 4):
                    total = total + prod[t, m, pl.ds(4 * r + i, DATES, stride=8), :]
                for q, part in enumerate(two_parts(total * scale)):
                    lanes = 128 * (2 * t + q)
                    stack[pl.ds(DATES * g, DATES), lanes : lanes + 128] = part

    lane = lax.broadcasted_iota(jnp.int32, (512, 128), 0)
    place = lax.broadcasted_iota(jnp.int32, (512, 128), 1)
    sums = ((lane // 256) * 8 + (lane % 128) // 16 == place % 16).astype(jnp.bfloat16)
    out = jnp.dot(stack[...], sums, preferred_element_type=jnp.float32)
    found = [out[DATES * g : DATES * g + DATES, :] for g in range(4 * SLOTS + 2)]

    column = lax.broadcasted_iota(jnp.int32, (DATES, 2 * DATES), 1) % DATES
    date = lax.broadcasted_iota(jnp.int32, (DATES, 2 * DATES), 0)
    pick = []
    for j in range(SLOTS):
        offset = jnp.broadcast_to(offs[:, j : j + 1], (DATES, 2 * DATES))
        pick.append(((column == date + offset) & (offset > 0)).astype(jnp.float32))
    own = [jnp.concatenate(two_parts(value), axis=0) for value in found[4 * SLOTS :]]
    partner = jnp.dot(
        jnp.concatenate(pick, axis=0).astype(jnp.bfloat16),
        jnp.concatenate(own, axis=1),
        preferred_element_type=jnp.float32,
    )
    picked = [
        partner[DATES * j : DATES * j + DATES, 128 * r : 128 * r + 128] for j in range(SLOTS) for r in range(2)
    ]
    found = found[: 4 * SLOTS] + picked + found[4 * SLOTS :]

    lanes = lax.broadcasted_iota(jnp.int32, (DATES, 128), 1)
    for k in range(4):
        block = jnp.zeros((DATES, 128), jnp.float32)
        for g in range(8 * k, min(8 * k + 8, GROUPS)):
            block = jnp.where(lanes // 16 == g - 8 * k, found[g], block)
        looks_ref[pl.ds(k, DATES, stride=4), :] = block


def local_looks(offsets, tiles):
    return pl.pallas_call(
        looks_kernel,
        out_shape=pltpu.VMEM((4 * DATES, 128), jnp.float32),
        in_specs=[pl.BlockSpec(memory_space=pltpu.SMEM), VMEM, VMEM],
        out_specs=VMEM,
        scratch_shapes=[
            pltpu.VMEM((2, 2 * SLOTS + 1, 8 * DATES, 128), jnp.float32),
            pltpu.VMEM(((4 * SLOTS + 2) * DATES, 512), jnp.bfloat16),
        ],
        name="looks",
    )(offsets, in_vmem(offsets), in_vmem(tiles))


def with_edge_kernel(looks_ref, edge_ref, out_ref):
    rows = pl.ds(3, DATES, stride=4)
    out_ref[rows, :] = looks_ref[rows, :] + edge_ref[...]


def with_edge(looks, edge):
    return pl.pallas_call(
        with_edge_kernel,
        out_shape=pltpu.VMEM((4 * DATES, 128), jnp.float32),
        in_specs=[VMEM, VMEM],
        out_specs=VMEM,
        input_output_aliases={0: 0},
        name="with_edge",
    )(in_vmem(looks), in_vmem(edge))


def finish_kernel(offs_ref, looks_ref, inter_out, coh_out, inter_ref, coh_ref, sems):
    odd = odd_col()
    lanes = lax.broadcasted_iota(jnp.int32, (16, 128), 1)
    blocks = [
        [looks_ref[pl.ds(4 * jnp.bitwise_xor(odd, half) + k, 16, stride=8), :] for k in range(4)]
        for half in range(2)
    ]

    second = [pltpu.roll(block, 16, 1) for block in blocks[1]]
    halos = jnp.where(lanes < HALO_LANE + 32, blocks[0][3], pltpu.roll(blocks[1][3], 33, 1))

    def cells(m, r):
        g = 2 * m + r
        k, at = g // 8, 16 * (g % 8)
        both = jnp.where(lanes // 16 == g % 8, blocks[0][k], second[k])
        halo = pltpu.roll(halos, (127 - HALO_LANE - g) % 128, 1)
        return jnp.where(lanes < 32, pltpu.roll(both, (128 - at) % 128, 1), halo)

    row = lax.broadcasted_iota(jnp.int32, (16, 128), 0)

    def window(m):
        across = []
        for r in range(2):
            value = cells(m, r)
            if m < 2 * SLOTS:
                inter_ref[m // SLOTS, 0, m % SLOTS, pl.ds(r, 16, stride=2), :] = value[:, :32]
            across.append(value + pltpu.roll(value, 1, 1) + pltpu.roll(value, 127, 1))
        both = across[0] + across[1]
        above = jnp.where(row == 0, 0.0, pltpu.roll(across[1], 1, 0))
        below = jnp.where(row == 15, 0.0, pltpu.roll(across[0], 15, 0))
        return both + above, both + below

    copies = []
    own = window(MAPS - 1)
    lives = (offs_ref[pl.ds(lax.axis_index("date"), 1), :] > 0).astype(jnp.float32)
    for j in range(SLOTS):
        live = jnp.broadcast_to(lives[:, j : j + 1], (16, 128))
        real, imag = window(j), window(SLOTS + j)
        for p in range(2):
            copy = pltpu.make_async_copy(inter_ref.at[p, 0, j], inter_out.at[p, 0, j], sems.at[p, j])
            copy.start()
            copies.append(copy)
        partner = window(2 * SLOTS + j)
        for r in range(2):
            magnitude = jnp.sqrt(real[r] * real[r] + imag[r] * imag[r])
            value = magnitude / (jnp.sqrt((own[r] * live) * partner[r]) + epsilon)
            coh_ref[0, j, pl.ds(r, 16, stride=2), :] = value[:, :32]
        last = pltpu.make_async_copy(coh_ref.at[0, j], coh_out.at[0, j], sems.at[2, j])
        last.start()
        copies.append(last)
    for copy in copies:
        copy.wait()


def finish(offsets, looks):
    return pl.pallas_call(
        finish_kernel,
        out_shape=(
            jax.ShapeDtypeStruct((2, 1, SLOTS, 32, 32), jnp.float32),
            jax.ShapeDtypeStruct((1, SLOTS, 32, 32), jnp.float32),
        ),
        in_specs=[VMEM, VMEM],
        out_specs=(ANY, ANY),
        scratch_shapes=[
            pltpu.VMEM((2, 1, SLOTS, 32, 32), jnp.float32),
            pltpu.VMEM((1, SLOTS, 32, 32), jnp.float32),
            pltpu.SemaphoreType.DMA((3, SLOTS)),
        ],
        name="finish",
    )(in_vmem(offsets), in_vmem(looks))


def edge_pairs(dates, cols):
    pairs = []
    for c in range(1, cols):
        for d in range(c % 2, dates, 2):
            here, there = d * cols + c, d * cols + c - 1
            pairs += [(here, there), (there, here)]
    return pairs


def shards(slc, offsets):
    tiles, offsets = pieces(slc, offsets)
    tiles = lax.all_to_all(tiles.reshape(DATES, 32, 128), "date", 0, 0, tiled=True)
    tiles = tiles.reshape(32 * DATES, 128)
    edge = edge_looks(offsets, tiles)
    edge = lax.ppermute(edge, ("date", "col"), edge_pairs(DATES, lax.axis_size("col")))
    looks = with_edge(local_looks(offsets, tiles), edge)
    looks = lax.all_to_all(looks.reshape(DATES, 4, 128), "date", 0, 0, tiled=True)
    return finish(offsets, looks.reshape(4 * DATES, 128))


def solution(mesh):
    placed = (P(None, "date", None, "col"), P())
    return jax.shard_map(
        shards,
        mesh=mesh,
        in_specs=placed,
        out_specs=(P(None, "date", None, None, "col"), P("date", None, None, "col")),
        check_vma=False,
    )
```

```python
import jax
import jax.numpy as jnp
from jax import lax
from jax.experimental import pallas as pl
from jax.experimental.pallas import tpu as pltpu
from jax.sharding import PartitionSpec as P

SLOTS = 4
DATES = 32
MAX_OFFSET = 6
MAPS = 3 * SLOTS + 1
GROUPS = 2 * MAPS
HALO_LANE = 32

epsilon = 1e-06

VMEM = pl.BlockSpec(memory_space=pltpu.VMEM)
ANY = pl.BlockSpec(memory_space=pl.ANY)


def in_vmem(value):
    return pltpu.with_memory_space_constraint(value, pltpu.VMEM)


def odd_col():
    return lax.rem(lax.axis_index("col"), 2)


def own_half():
    return lax.rem(lax.axis_index("date") + lax.axis_index("col"), 2)


def two_parts(value):
    high = value.astype(jnp.bfloat16)
    return high, (value - high.astype(jnp.float32)).astype(jnp.bfloat16)


def pieces_kernel(slc_ref, slots_ref, out_ref, offs_ref, planes, slots, sems, slots_sem):
    odd = odd_col()
    first = pltpu.make_async_copy(slots_ref, slots, slots_sem)
    first.start()
    copies = [pltpu.make_async_copy(slc_ref.at[p], planes.at[p], sems.at[p]) for p in range(2)]
    for copy in copies:
        copy.start()
    first.wait()
    offs_ref[...] = slots[...].T
    for p, copy in enumerate(copies):
        copy.wait()
        for block in range(16):
            for half in range(2):
                out_ref[block, jnp.bitwise_xor(odd, half), p] = planes[p, block, half]


def pieces(slc, offsets):
    tiles = slc.reshape(2, 16, 8, 2, 2, 128).transpose(0, 1, 3, 4, 2, 5)
    return pl.pallas_call(
        pieces_kernel,
        out_shape=(
            pltpu.VMEM((16, 2, 2, 2, 8, 128), jnp.float32),
            pltpu.VMEM((DATES, SLOTS), jnp.int32),
        ),
        in_specs=[ANY, ANY],
        out_specs=(VMEM, VMEM),
        scratch_shapes=[
            pltpu.VMEM((2, 16, 2, 2, 8, 128), jnp.float32),
            pltpu.VMEM((SLOTS, DATES), jnp.int32),
            pltpu.SemaphoreType.DMA((2,)),
            pltpu.SemaphoreType.DMA,
        ],
        name="pieces",
    )(tiles, offsets.T)


def edge_kernel(offs_ref, tiles_ref, edge_ref, tiles, shifted, stack):
    half = own_half()
    lanes = lax.broadcasted_iota(jnp.int32, (DATES, 128), 1)
    packed = []
    for p in range(2):
        for d in range(DATES):
            tile = tiles_ref[pl.ds(pl.multiple_of(32 * d + 16 * p + 8 * half, 8), 8), :]
            tiles[p, 8 * d : 8 * d + 8, :] = tile
        value = jnp.zeros((DATES, 128), jnp.float32)
        for i in range(8):
            row = tiles[p, pl.ds(i, DATES, stride=8), :]
            value = jnp.where(lanes // 16 == i, pltpu.roll(row, 16 * (half + i), 1), value)
        packed.append(value)
    for p in range(2):
        shifted[p, 0:DATES, :] = packed[p]
        shifted[p, DATES : DATES + 8, :] = jnp.zeros((8, 128), jnp.float32)
    offs = offs_ref[...]
    for top in range(0, DATES, 16):
        rows = slice(top, top + 16)
        real, imag = packed[0][rows, :], packed[1][rows, :]
        offset = [jnp.broadcast_to(offs[rows, j : j + 1], (16, 128)) for j in range(SLOTS)]
        partner = [[jnp.zeros((16, 128), jnp.float32)] * 2 for j in range(SLOTS)]
        for step in range(1, MAX_OFFSET + 1):
            later = [shifted[p, top + step : top + step + 16, :] for p in range(2)]
            for j in range(SLOTS):
                here = offset[j] == step
                partner[j] = [jnp.where(here, later[p], partner[j][p]) for p in range(2)]
        looks = [real * b[0] + imag * b[1] for b in partner]
        looks += [imag * b[0] - real * b[1] for b in partner]
        looks += [b[0] * b[0] + b[1] * b[1] for b in partner]
        looks += [real * real + imag * imag]
        for m in range(MAPS):
            for q, part in enumerate(two_parts(looks[m])):
                stack[DATES * m + top : DATES * m + top + 16, 128 * q : 128 * q + 128] = part
    lane = lax.broadcasted_iota(jnp.int32, (128, 128), 0)
    place = lax.broadcasted_iota(jnp.int32, (128, 128), 1)
    sums = jnp.where(lane // 64 == place % 2, 1.0 / 64.0, 0.0).astype(jnp.bfloat16)
    sums = jnp.concatenate([sums, sums], axis=0)
    out = jnp.dot(stack[...], sums, preferred_element_type=jnp.float32)
    edge = jnp.zeros((DATES, 128), jnp.float32)
    for m in range(MAPS):
        edge = jnp.where((lanes - HALO_LANE) // 2 == m, out[DATES * m : DATES * m + DATES, :], edge)
    edge_ref[...] = jnp.where(lanes >= HALO_LANE, edge, 0.0)


def edge_looks(offsets, tiles):
    return pl.pallas_call(
        edge_kernel,
        out_shape=pltpu.VMEM((DATES, 128), jnp.float32),
        in_specs=[VMEM, VMEM],
        out_specs=VMEM,
        scratch_shapes=[
            pltpu.VMEM((2, 8 * DATES, 128), jnp.float32),
            pltpu.VMEM((2, DATES + 8, 128), jnp.float32),
            pltpu.VMEM((MAPS * DATES, 256), jnp.bfloat16),
        ],
        name="edge_looks",
    )(in_vmem(offsets), in_vmem(tiles))


def looks_kernel(offs_smem, offs_ref, tiles_ref, looks_ref, prod, stack):
    def tile(d, p, t):
        return tiles_ref[pl.ds(pl.multiple_of(d * 32 + 16 * p + 8 * t, 8), 8), :]

    def powers(d, carry):
        for t in range(2):
            real, imag = tile(d, 0, t), tile(d, 1, t)
            prod[t, 2 * SLOTS, pl.ds(pl.multiple_of(d * 8, 8), 8), :] = real * real + imag * imag
        return carry

    lax.fori_loop(0, DATES, powers, 0, unroll=4)

    def pairs(d, carry):
        rows = pl.ds(pl.multiple_of(d * 8, 8), 8)
        for t in range(2):
            master_real, master_imag = tile(d, 0, t), tile(d, 1, t)
            for j in range(SLOTS):
                p = jnp.minimum(d + offs_smem[d, j], DATES - 1)
                partner_real, partner_imag = tile(p, 0, t), tile(p, 1, t)
                prod[t, j, rows, :] = master_real * partner_real + master_imag * partner_imag
                prod[t, SLOTS + j, rows, :] = master_imag * partner_real - master_real * partner_imag
        return carry

    lax.fori_loop(0, DATES, pairs, 0, unroll=2)

    offs = offs_ref[...]
    live = (offs > 0).astype(jnp.float32) / 64.0
    lives = [jnp.broadcast_to(live[:, j : j + 1], (DATES, 128)) for j in range(SLOTS)]
    for m in range(2 * SLOTS + 1):
        scale = lives[m % SLOTS] if m < 2 * SLOTS else 1.0 / 64.0
        for r in range(2):
            g = 2 * m + r
            for t in range(2):
                total = prod[t, m, pl.ds(4 * r, DATES, stride=8), :]
                for i in range(1, 4):
                    total = total + prod[t, m, pl.ds(4 * r + i, DATES, stride=8), :]
                for q, part in enumerate(two_parts(total * scale)):
                    lanes = 128 * (2 * t + q)
                    stack[pl.ds(DATES * g, DATES), lanes : lanes + 128] = part

    lane = lax.broadcasted_iota(jnp.int32, (512, 128), 0)
    place = lax.broadcasted_iota(jnp.int32, (512, 128), 1)
    sums = ((lane // 256) * 8 + (lane % 128) // 16 == place % 16).astype(jnp.bfloat16)
    out = jnp.dot(stack[...], sums, preferred_element_type=jnp.float32)
    found = [out[DATES * g : DATES * g + DATES, :] for g in range(4 * SLOTS + 2)]

    column = lax.broadcasted_iota(jnp.int32, (DATES, 2 * DATES), 1) % DATES
    date = lax.broadcasted_iota(jnp.int32, (DATES, 2 * DATES), 0)
    pick = []
    for j in range(SLOTS):
        offset = jnp.broadcast_to(offs[:, j : j + 1], (DATES, 2 * DATES))
        pick.append(((column == date + offset) & (offset > 0)).astype(jnp.float32))
    own = [jnp.concatenate(two_parts(value), axis=0) for value in found[4 * SLOTS :]]
    partner = jnp.dot(
        jnp.concatenate(pick, axis=0).astype(jnp.bfloat16),
        jnp.concatenate(own, axis=1),
        preferred_element_type=jnp.float32,
    )
    picked = [
        partner[DATES * j : DATES * j + DATES, 128 * r : 128 * r + 128] for j in range(SLOTS) for r in range(2)
    ]
    found = found[: 4 * SLOTS] + picked + found[4 * SLOTS :]

    lanes = lax.broadcasted_iota(jnp.int32, (DATES, 128), 1)
    for k in range(4):
        block = jnp.zeros((DATES, 128), jnp.float32)
        for g in range(8 * k, min(8 * k + 8, GROUPS)):
            block = jnp.where(lanes // 16 == g - 8 * k, found[g], block)
        looks_ref[pl.ds(k, DATES, stride=4), :] = block


def local_looks(offsets, tiles):
    return pl.pallas_call(
        looks_kernel,
        out_shape=pltpu.VMEM((4 * DATES, 128), jnp.float32),
        in_specs=[pl.BlockSpec(memory_space=pltpu.SMEM), VMEM, VMEM],
        out_specs=VMEM,
        scratch_shapes=[
            pltpu.VMEM((2, 2 * SLOTS + 1, 8 * DATES, 128), jnp.float32),
            pltpu.VMEM(((4 * SLOTS + 2) * DATES, 512), jnp.bfloat16),
        ],
        name="looks",
    )(offsets, in_vmem(offsets), in_vmem(tiles))


def with_edge_kernel(looks_ref, edge_ref, out_ref):
    rows = pl.ds(3, DATES, stride=4)
    out_ref[rows, :] = looks_ref[rows, :] + edge_ref[...]


def with_edge(looks, edge):
    return pl.pallas_call(
        with_edge_kernel,
        out_shape=pltpu.VMEM((4 * DATES, 128), jnp.float32),
        in_specs=[VMEM, VMEM],
        out_specs=VMEM,
        input_output_aliases={0: 0},
        name="with_edge",
    )(in_vmem(looks), in_vmem(edge))


def finish_kernel(offs_ref, looks_ref, inter_out, coh_out, inter_ref, coh_ref, sems):
    odd = odd_col()
    lanes = lax.broadcasted_iota(jnp.int32, (16, 128), 1)
    blocks = [
        [looks_ref[pl.ds(4 * jnp.bitwise_xor(odd, half) + k, 16, stride=8), :] for k in range(4)]
        for half in range(2)
    ]

    second = [pltpu.roll(block, 16, 1) for block in blocks[1]]
    halos = jnp.where(lanes < HALO_LANE + 32, blocks[0][3], pltpu.roll(blocks[1][3], 33, 1))

    def cells(m, r):
        g = 2 * m + r
        k, at = g // 8, 16 * (g % 8)
        both = jnp.where(lanes // 16 == g % 8, blocks[0][k], second[k])
        halo = pltpu.roll(halos, (127 - HALO_LANE - g) % 128, 1)
        return jnp.where(lanes < 32, pltpu.roll(both, (128 - at) % 128, 1), halo)

    row = lax.broadcasted_iota(jnp.int32, (16, 128), 0)

    def window(m):
        across = []
        for r in range(2):
            value = cells(m, r)
            if m < 2 * SLOTS:
                inter_ref[m // SLOTS, 0, m % SLOTS, pl.ds(r, 16, stride=2), :] = value[:, :32]
            across.append(value + pltpu.roll(value, 1, 1) + pltpu.roll(value, 127, 1))
        both = across[0] + across[1]
        above = jnp.where(row == 0, 0.0, pltpu.roll(across[1], 1, 0))
        below = jnp.where(row == 15, 0.0, pltpu.roll(across[0], 15, 0))
        return both + above, both + below

    copies = []
    own = window(MAPS - 1)
    lives = (offs_ref[pl.ds(lax.axis_index("date"), 1), :] > 0).astype(jnp.float32)
    for j in range(SLOTS):
        live = jnp.broadcast_to(lives[:, j : j + 1], (16, 128))
        real, imag = window(j), window(SLOTS + j)
        both = pltpu.make_async_copy(inter_ref.at[:, 0, j], inter_out.at[:, 0, j], sems.at[0, j])
        both.start()
        copies.append(both)
        partner = window(2 * SLOTS + j)
        for r in range(2):
            magnitude = jnp.sqrt(real[r] * real[r] + imag[r] * imag[r])
            value = magnitude / (jnp.sqrt((own[r] * live) * partner[r]) + epsilon)
            coh_ref[0, j, pl.ds(r, 16, stride=2), :] = value[:, :32]
        last = pltpu.make_async_copy(coh_ref.at[0, j], coh_out.at[0, j], sems.at[1, j])
        last.start()
        copies.append(last)
    for copy in copies:
        copy.wait()


def finish(offsets, looks):
    return pl.pallas_call(
        finish_kernel,
        out_shape=(
            jax.ShapeDtypeStruct((2, 1, SLOTS, 32, 32), jnp.float32),
            jax.ShapeDtypeStruct((1, SLOTS, 32, 32), jnp.float32),
        ),
        in_specs=[VMEM, VMEM],
        out_specs=(ANY, ANY),
        scratch_shapes=[
            pltpu.VMEM((2, 1, SLOTS, 32, 32), jnp.float32),
            pltpu.VMEM((1, SLOTS, 32, 32), jnp.float32),
            pltpu.SemaphoreType.DMA((2, SLOTS)),
        ],
        name="finish",
    )(in_vmem(offsets), in_vmem(looks))


def edge_pairs(dates, cols):
    pairs = []
    for c in range(1, cols):
        for d in range(c % 2, dates, 2):
            here, there = d * cols + c, d * cols + c - 1
            pairs += [(here, there), (there, here)]
    return pairs


def shards(slc, offsets):
    tiles, offsets = pieces(slc, offsets)
    tiles = lax.all_to_all(tiles.reshape(DATES, 32, 128), "date", 0, 0, tiled=True)
    tiles = tiles.reshape(32 * DATES, 128)
    edge = edge_looks(offsets, tiles)
    edge = lax.ppermute(edge, ("date", "col"), edge_pairs(DATES, lax.axis_size("col")))
    looks = with_edge(local_looks(offsets, tiles), edge)
    looks = lax.all_to_all(looks.reshape(DATES, 4, 128), "date", 0, 0, tiled=True)
    return finish(offsets, looks.reshape(4 * DATES, 128))


def solution(mesh):
    placed = (P(None, "date", None, "col"), P())
    return jax.shard_map(
        shards,
        mesh=mesh,
        in_specs=placed,
        out_specs=(P(None, "date", None, None, "col"), P("date", None, None, "col")),
        check_vma=False,
    )
```

```python
import jax
import jax.numpy as jnp
from jax import lax
from jax.experimental import pallas as pl
from jax.experimental.pallas import tpu as pltpu
from jax.sharding import PartitionSpec as P

SLOTS = 4
DATES = 32
MAX_OFFSET = 6
MAPS = 3 * SLOTS + 1
GROUPS = 2 * MAPS
HALO_LANE = 32

epsilon = 1e-06

VMEM = pl.BlockSpec(memory_space=pltpu.VMEM)
ANY = pl.BlockSpec(memory_space=pl.ANY)


def in_vmem(value):
    return pltpu.with_memory_space_constraint(value, pltpu.VMEM)


def odd_col():
    return lax.rem(lax.axis_index("col"), 2)


def own_half():
    return lax.rem(lax.axis_index("date") + lax.axis_index("col"), 2)


def two_parts(value):
    high = value.astype(jnp.bfloat16)
    return high, (value - high.astype(jnp.float32)).astype(jnp.bfloat16)


def pieces_kernel(slc_ref, slots_ref, out_ref, offs_ref, planes, slots, sems, slots_sem):
    odd = odd_col()
    first = pltpu.make_async_copy(slots_ref, slots, slots_sem)
    copies = [pltpu.make_async_copy(slc_ref.at[p], planes.at[p], sems.at[p]) for p in range(2)]
    for copy in copies:
        copy.start()
    first.start()
    first.wait()
    offs_ref[...] = slots[...].T
    for p, copy in enumerate(copies):
        copy.wait()
        for block in range(16):
            for half in range(2):
                out_ref[block, jnp.bitwise_xor(odd, half), p] = planes[p, block, half]


def pieces(slc, offsets):
    tiles = slc.reshape(2, 16, 8, 2, 2, 128).transpose(0, 1, 3, 4, 2, 5)
    return pl.pallas_call(
        pieces_kernel,
        out_shape=(
            pltpu.VMEM((16, 2, 2, 2, 8, 128), jnp.float32),
            pltpu.VMEM((DATES, SLOTS), jnp.int32),
        ),
        in_specs=[ANY, ANY],
        out_specs=(VMEM, VMEM),
        scratch_shapes=[
            pltpu.VMEM((2, 16, 2, 2, 8, 128), jnp.float32),
            pltpu.VMEM((SLOTS, DATES), jnp.int32),
            pltpu.SemaphoreType.DMA((2,)),
            pltpu.SemaphoreType.DMA,
        ],
        name="pieces",
    )(tiles, offsets.T)


def edge_kernel(offs_ref, tiles_ref, edge_ref, tiles, shifted, stack):
    half = own_half()
    lanes = lax.broadcasted_iota(jnp.int32, (DATES, 128), 1)
    packed = []
    for p in range(2):
        for d in range(DATES):
            tile = tiles_ref[pl.ds(pl.multiple_of(32 * d + 16 * p + 8 * half, 8), 8), :]
            tiles[p, 8 * d : 8 * d + 8, :] = tile
        value = jnp.zeros((DATES, 128), jnp.float32)
        for i in range(8):
            row = tiles[p, pl.ds(i, DATES, stride=8), :]
            value = jnp.where(lanes // 16 == i, pltpu.roll(row, 16 * (half + i), 1), value)
        packed.append(value)
    for p in range(2):
        shifted[p, 0:DATES, :] = packed[p]
        shifted[p, DATES : DATES + 8, :] = jnp.zeros((8, 128), jnp.float32)
    offs = offs_ref[...]
    for top in range(0, DATES, 16):
        rows = slice(top, top + 16)
        real, imag = packed[0][rows, :], packed[1][rows, :]
        offset = [jnp.broadcast_to(offs[rows, j : j + 1], (16, 128)) for j in range(SLOTS)]
        partner = [[jnp.zeros((16, 128), jnp.float32)] * 2 for j in range(SLOTS)]
        for step in range(1, MAX_OFFSET + 1):
            later = [shifted[p, top + step : top + step + 16, :] for p in range(2)]
            for j in range(SLOTS):
                here = offset[j] == step
                partner[j] = [jnp.where(here, later[p], partner[j][p]) for p in range(2)]
        looks = [real * b[0] + imag * b[1] for b in partner]
        looks += [imag * b[0] - real * b[1] for b in partner]
        looks += [b[0] * b[0] + b[1] * b[1] for b in partner]
        looks += [real * real + imag * imag]
        for m in range(MAPS):
            for q, part in enumerate(two_parts(looks[m])):
                stack[DATES * m + top : DATES * m + top + 16, 128 * q : 128 * q + 128] = part
    lane = lax.broadcasted_iota(jnp.int32, (128, 128), 0)
    place = lax.broadcasted_iota(jnp.int32, (128, 128), 1)
    sums = jnp.where(lane // 64 == place % 2, 1.0 / 64.0, 0.0).astype(jnp.bfloat16)
    sums = jnp.concatenate([sums, sums], axis=0)
    out = jnp.dot(stack[...], sums, preferred_element_type=jnp.float32)
    edge = jnp.zeros((DATES, 128), jnp.float32)
    for m in range(MAPS):
        edge = jnp.where((lanes - HALO_LANE) // 2 == m, out[DATES * m : DATES * m + DATES, :], edge)
    edge_ref[...] = edge


def edge_looks(offsets, tiles):
    return pl.pallas_call(
        edge_kernel,
        out_shape=pltpu.VMEM((DATES, 128), jnp.float32),
        in_specs=[VMEM, VMEM],
        out_specs=VMEM,
        scratch_shapes=[
            pltpu.VMEM((2, 8 * DATES, 128), jnp.float32),
            pltpu.VMEM((2, DATES + 8, 128), jnp.float32),
            pltpu.VMEM((MAPS * DATES, 256), jnp.bfloat16),
        ],
        name="edge_looks",
    )(in_vmem(offsets), in_vmem(tiles))


def looks_kernel(offs_smem, offs_ref, tiles_ref, looks_ref, prod, stack):
    def tile(d, p, t):
        return tiles_ref[pl.ds(pl.multiple_of(d * 32 + 16 * p + 8 * t, 8), 8), :]

    def powers(d, carry):
        for t in range(2):
            real, imag = tile(d, 0, t), tile(d, 1, t)
            prod[t, 2 * SLOTS, pl.ds(pl.multiple_of(d * 8, 8), 8), :] = real * real + imag * imag
        return carry

    lax.fori_loop(0, DATES, powers, 0, unroll=4)

    def pairs(d, carry):
        rows = pl.ds(pl.multiple_of(d * 8, 8), 8)
        for t in range(2):
            master_real, master_imag = tile(d, 0, t), tile(d, 1, t)
            for j in range(SLOTS):
                p = jnp.minimum(d + offs_smem[d, j], DATES - 1)
                partner_real, partner_imag = tile(p, 0, t), tile(p, 1, t)
                prod[t, j, rows, :] = master_real * partner_real + master_imag * partner_imag
                prod[t, SLOTS + j, rows, :] = master_imag * partner_real - master_real * partner_imag
        return carry

    lax.fori_loop(0, DATES, pairs, 0, unroll=2)

    offs = offs_ref[...]
    live = (offs > 0).astype(jnp.float32) / 64.0
    lives = [jnp.broadcast_to(live[:, j : j + 1], (DATES, 128)) for j in range(SLOTS)]
    for m in range(2 * SLOTS + 1):
        scale = lives[m % SLOTS] if m < 2 * SLOTS else 1.0 / 64.0
        for r in range(2):
            g = 2 * m + r
            for t in range(2):
                total = prod[t, m, pl.ds(4 * r, DATES, stride=8), :]
                for i in range(1, 4):
                    total = total + prod[t, m, pl.ds(4 * r + i, DATES, stride=8), :]
                for q, part in enumerate(two_parts(total * scale)):
                    lanes = 128 * (2 * t + q)
                    stack[pl.ds(DATES * g, DATES), lanes : lanes + 128] = part

    lane = lax.broadcasted_iota(jnp.int32, (512, 128), 0)
    place = lax.broadcasted_iota(jnp.int32, (512, 128), 1)
    sums = ((lane // 256) * 8 + (lane % 128) // 16 == place % 16).astype(jnp.bfloat16)
    out = jnp.dot(stack[...], sums, preferred_element_type=jnp.float32)
    found = [out[DATES * g : DATES * g + DATES, :] for g in range(4 * SLOTS + 2)]

    column = lax.broadcasted_iota(jnp.int32, (DATES, 2 * DATES), 1) % DATES
    date = lax.broadcasted_iota(jnp.int32, (DATES, 2 * DATES), 0)
    pick = []
    for j in range(SLOTS):
        offset = jnp.broadcast_to(offs[:, j : j + 1], (DATES, 2 * DATES))
        pick.append(((column == date + offset) & (offset > 0)).astype(jnp.float32))
    own = [jnp.concatenate(two_parts(value), axis=0) for value in found[4 * SLOTS :]]
    partner = jnp.dot(
        jnp.concatenate(pick, axis=0).astype(jnp.bfloat16),
        jnp.concatenate(own, axis=1),
        preferred_element_type=jnp.float32,
    )
    picked = [
        partner[DATES * j : DATES * j + DATES, 128 * r : 128 * r + 128] for j in range(SLOTS) for r in range(2)
    ]
    found = found[: 4 * SLOTS] + picked + found[4 * SLOTS :]

    lanes = lax.broadcasted_iota(jnp.int32, (DATES, 128), 1)
    for k in range(4):
        block = jnp.zeros((DATES, 128), jnp.float32)
        for g in range(8 * k, min(8 * k + 8, GROUPS)):
            block = jnp.where(lanes // 16 == g - 8 * k, found[g], block)
        looks_ref[pl.ds(k, DATES, stride=4), :] = block


def local_looks(offsets, tiles):
    return pl.pallas_call(
        looks_kernel,
        out_shape=pltpu.VMEM((4 * DATES, 128), jnp.float32),
        in_specs=[pl.BlockSpec(memory_space=pltpu.SMEM), VMEM, VMEM],
        out_specs=VMEM,
        scratch_shapes=[
            pltpu.VMEM((2, 2 * SLOTS + 1, 8 * DATES, 128), jnp.float32),
            pltpu.VMEM(((4 * SLOTS + 2) * DATES, 512), jnp.bfloat16),
        ],
        name="looks",
    )(offsets, in_vmem(offsets), in_vmem(tiles))


def with_edge_kernel(looks_ref, edge_ref, out_ref):
    rows = pl.ds(3, DATES, stride=4)
    out_ref[rows, :] = looks_ref[rows, :] + edge_ref[...]


def with_edge(looks, edge):
    return pl.pallas_call(
        with_edge_kernel,
        out_shape=pltpu.VMEM((4 * DATES, 128), jnp.float32),
        in_specs=[VMEM, VMEM],
        out_specs=VMEM,
        input_output_aliases={0: 0},
        name="with_edge",
    )(in_vmem(looks), in_vmem(edge))


def finish_kernel(offs_ref, looks_ref, inter_out, coh_out, inter_ref, coh_ref, sems):
    odd = odd_col()
    lanes = lax.broadcasted_iota(jnp.int32, (16, 128), 1)
    blocks = [
        [looks_ref[pl.ds(4 * jnp.bitwise_xor(odd, half) + k, 16, stride=8), :] for k in range(4)]
        for half in range(2)
    ]

    second = [pltpu.roll(block, 16, 1) for block in blocks[1]]
    halos = jnp.where(lanes < HALO_LANE + 32, blocks[0][3], pltpu.roll(blocks[1][3], 33, 1))

    def cells(m, r):
        g = 2 * m + r
        k, at = g // 8, 16 * (g % 8)
        both = jnp.where(lanes // 16 == g % 8, blocks[0][k], second[k])
        halo = pltpu.roll(halos, (127 - HALO_LANE - g) % 128, 1)
        return jnp.where(lanes < 32, pltpu.roll(both, (128 - at) % 128, 1), halo)

    row = lax.broadcasted_iota(jnp.int32, (16, 128), 0)

    def window(m):
        across = []
        for r in range(2):
            value = cells(m, r)
            if m < 2 * SLOTS:
                inter_ref[m // SLOTS, 0, m % SLOTS, pl.ds(r, 16, stride=2), :] = value[:, :32]
            across.append(value + pltpu.roll(value, 1, 1) + pltpu.roll(value, 127, 1))
        both = across[0] + across[1]
        above = jnp.where(row == 0, 0.0, pltpu.roll(across[1], 1, 0))
        below = jnp.where(row == 15, 0.0, pltpu.roll(across[0], 15, 0))
        return both + above, both + below

    copies = []
    own = window(MAPS - 1)
    lives = (offs_ref[pl.ds(lax.axis_index("date"), 1), :] > 0).astype(jnp.float32)
    for j in range(SLOTS):
        live = jnp.broadcast_to(lives[:, j : j + 1], (16, 128))
        real, imag = window(j), window(SLOTS + j)
        both = pltpu.make_async_copy(inter_ref.at[:, 0, j], inter_out.at[:, 0, j], sems.at[0, j])
        both.start()
        copies.append(both)
        partner = window(2 * SLOTS + j)
        for r in range(2):
            magnitude = jnp.sqrt(real[r] * real[r] + imag[r] * imag[r])
            value = magnitude / (jnp.sqrt((own[r] * live) * partner[r]) + epsilon)
            coh_ref[0, j, pl.ds(r, 16, stride=2), :] = value[:, :32]
        last = pltpu.make_async_copy(coh_ref.at[0, j], coh_out.at[0, j], sems.at[1, j])
        last.start()
        copies.append(last)
    for copy in copies:
        copy.wait()


def finish(offsets, looks):
    return pl.pallas_call(
        finish_kernel,
        out_shape=(
            jax.ShapeDtypeStruct((2, 1, SLOTS, 32, 32), jnp.float32),
            jax.ShapeDtypeStruct((1, SLOTS, 32, 32), jnp.float32),
        ),
        in_specs=[VMEM, VMEM],
        out_specs=(ANY, ANY),
        scratch_shapes=[
            pltpu.VMEM((2, 1, SLOTS, 32, 32), jnp.float32),
            pltpu.VMEM((1, SLOTS, 32, 32), jnp.float32),
            pltpu.SemaphoreType.DMA((2, SLOTS)),
        ],
        name="finish",
    )(in_vmem(offsets), in_vmem(looks))


def edge_pairs(dates, cols):
    pairs = []
    for c in range(1, cols):
        for d in range(c % 2, dates, 2):
            here, there = d * cols + c, d * cols + c - 1
            pairs += [(here, there), (there, here)]
    return pairs


def shards(slc, offsets):
    tiles, offsets = pieces(slc, offsets)
    tiles = lax.all_to_all(tiles.reshape(DATES, 32, 128), "date", 0, 0, tiled=True)
    tiles = tiles.reshape(32 * DATES, 128)
    edge = edge_looks(offsets, tiles)
    edge = lax.ppermute(edge, ("date", "col"), edge_pairs(DATES, lax.axis_size("col")))
    looks = with_edge(local_looks(offsets, tiles), edge)
    looks = lax.all_to_all(looks.reshape(DATES, 4, 128), "date", 0, 0, tiled=True)
    return finish(offsets, looks.reshape(4 * DATES, 128))


def solution(mesh):
    placed = (P(None, "date", None, "col"), P())
    return jax.shard_map(
        shards,
        mesh=mesh,
        in_specs=placed,
        out_specs=(P(None, "date", None, None, "col"), P("date", None, None, "col")),
        check_vma=False,
    )
```
